1024 devices in a mesh: seq: 32 (over y, x_hi), dp: 32 (over z, x_lo, core).
Axes of the slice: x: 8 (x_hi: 4, x_lo: 2; x = x_hi * 2 + x_lo), y: 8, z: 8, core: 2. Of those that a mesh axis runs over, the one named last changes fastest.
Arguments:
- queries: bfloat16 [262144, 1024], P(('dp', 'seq')), parts along dimension 0, may hold values from -6 to 6
- keys: bfloat16 [262144, 256], P(('dp', 'seq')), parts along dimension 0, may hold values from -6 to 6
- values: bfloat16 [262144, 256], P(('dp', 'seq')), parts along dimension 0, may hold values from -6 to 6
- out_grad: bfloat16 [262144, 1024], P(('dp', 'seq')), parts along dimension 0, may hold values from -6 to 6
- rand_blocks: int32 [4096, 3], P('dp'), parts along dimension 0, may hold values from 0 to 127, as said below
- global_blocks: int32 [64], P('dp'), parts along dimension 0, may hold values from 0 to 127, as said below
Outputs:
- out: bfloat16 [262144, 1024], P(('dp', 'seq')), parts along dimension 0
- query_grad: bfloat16 [262144, 1024], P(('dp', 'seq')), parts along dimension 0
- key_grad: bfloat16 [262144, 256], P(('dp', 'seq')), parts along dimension 0
- value_grad: bfloat16 [262144, 256], P(('dp', 'seq')), parts along dimension 0
The draws below stay inside these ranges and needn't reach their ends.
There are 32 independent parts, one for each index of `dp`. The reference program is written for one: setup_inputs(seed, part) draws one part's arguments, and reference() takes and returns one part's arrays. A program takes and returns all parts, laid end to end along the dimension named above; each array names one. Nothing has to cross between parts.
Inputs may be any that keep to these rules, and one draw needn't show every extreme that they name: `rand_blocks`: block j lies on index j // 4 of seq. For each index r of seq, the 12 entries of rows r * 4 to (r + 1) * 4 - 1 together with the 2 global blocks name blocks of no index more than 1 times, and blocks of some index exactly 1 times. `global_blocks`: the global blocks lie on different indices of seq.
All inputs are finite; a program needn't handle non-finite values.
Results may differ from the reference program's by a relative error of at most 0.011.
Values may be sent and summed in bfloat16 or wider, within the bound.
A program may use at most 32 MiB of HBM per device.

```python
import jax
import jax.numpy as jnp
from jax import lax

KVH = 2
HD = 128
BLOCK = 64
GLOB = 2
RAND = 3
QB = 4
GROUP = 4
QW = 1024
KW = 256
NB = 128
TOKENS = 8192
CAP = 1
N_SEQ = 32


def far_lists(key):
    cycle_size = NB // QB
    base = jax.random.fold_in(key, 11)
    owner_pick = jax.random.permutation(jax.random.fold_in(base, 1), cycle_size)[:GLOB]
    local_pick = jax.random.randint(jax.random.fold_in(base, 2), (GLOB,), 0, QB)
    global_ids = (owner_pick * QB + local_pick).astype(jnp.int32)
    slot_total = cycle_size * CAP
    reserved = jnp.zeros((slot_total,), jnp.int32).at[owner_pick * CAP].set(1)

    def one_device(sub_key):
        scores = jax.random.permutation(sub_key, slot_total)
        scores = scores + reserved * slot_total
        ordering = jnp.argsort(scores)
        chosen = ordering[:RAND * QB]
        owners = chosen // CAP
        local_ids = jax.random.randint(jax.random.fold_in(sub_key, 5), (RAND * QB,), 0, QB)
        return owners * QB + local_ids
    device_keys = jax.random.split(jax.random.fold_in(base, 3), cycle_size)
    rand_ids = jax.vmap(one_device)(device_keys).reshape(NB, RAND).astype(jnp.int32)
    return (rand_ids, global_ids)


def draw_rand_blocks(key, part):
    return far_lists(key)[0]


def draw_global_blocks(key, part):
    return far_lists(key)[1]


def base_field(key, columns):
    field = jnp.clip(jax.random.normal(jax.random.fold_in(key, 34), (TOKENS, columns), jnp.float32), -5.0, 5.0)
    return field


def draw_queries(key, part):
    field = base_field(jax.random.fold_in(key, 41), QW)
    return field.astype(jnp.bfloat16)


def draw_keys(key, part):
    field = base_field(jax.random.fold_in(key, 42), KW)
    return field.astype(jnp.bfloat16)


def block_levels(own_key, extent, shards, least, high):
    gain = 1.0
    for position, blocks in shards:
        draws = jax.random.uniform(jax.random.fold_in(jax.random.fold_in(own_key, 6), position), (blocks,), jnp.float32, least / len(shards), high / len(shards))
        gain = gain * jnp.repeat(jnp.exp(draws), extent[position] // blocks).reshape((-1,) + (1,) * (len(extent) - 1 - position))
    return gain


def gaussian(rng, extent, scale, most, cuts=(), kind=jnp.bfloat16):
    entries = scale * jax.random.normal(rng, extent, jnp.float32)
    if cuts:
        entries = entries * block_levels(rng, extent, cuts, -0.22, 0.18)
    return jnp.clip(entries, -most, most).astype(kind)


def setup_inputs(seed: int = 0, part: int = 0) -> dict:
    seeds = jax.random.split(jax.random.key(seed), 7)
    own_keys = jax.random.split(jax.random.fold_in(seeds[6], part), 7)
    queries = draw_queries(jax.random.fold_in(jax.random.fold_in(seeds[6], part), 71), part)
    keys = draw_keys(jax.random.fold_in(jax.random.fold_in(seeds[6], part), 71), part)
    values = gaussian(own_keys[2], (TOKENS, KW), 1.0, 6.0, ((0, 32),))
    out_grad = gaussian(own_keys[3], (TOKENS, QW), 1.0, 6.0, ((0, 32),))
    rand_blocks = draw_rand_blocks(jax.random.fold_in(jax.random.fold_in(seeds[6], part), 71), part)
    global_blocks = draw_global_blocks(jax.random.fold_in(jax.random.fold_in(seeds[6], part), 71), part)
    return dict(queries=queries, keys=keys, values=values, out_grad=out_grad, rand_blocks=rand_blocks, global_blocks=global_blocks)


def attend(inputs):
    query_block, key_set, grad_block = inputs
    rows = query_block.shape[0]
    scale = HD ** -0.5
    heads_q = query_block.astype(jnp.float32).reshape(rows, KVH, GROUP, HD)
    grads_q = grad_block.astype(jnp.float32).reshape(rows, KVH, GROUP, HD)
    keys_all = key_set[:, :, 0].astype(jnp.float32).reshape(-1, KVH, HD)
    values_all = key_set[:, :, 1].astype(jnp.float32).reshape(-1, KVH, HD)
    scores = jnp.einsum("qgjd,kgd->gjqk", heads_q, keys_all) * scale
    peak = jnp.max(scores, axis=-1, keepdims=True)
    expos = jnp.exp(scores - peak)
    probs = expos / jnp.sum(expos, axis=-1, keepdims=True)
    probs_b = probs.astype(jnp.bfloat16)
    attended = jnp.einsum("gjqk,kgd->qgjd", probs_b.astype(jnp.float32), values_all)
    delta = jnp.transpose(jnp.sum(grads_q * attended, axis=-1), (1, 2, 0))
    dprobs = jnp.einsum("qgjd,kgd->gjqk", grads_q, values_all)
    dscores = (probs * (dprobs - delta[..., None]) * scale).astype(jnp.bfloat16)
    qgrad = jnp.einsum("gjqk,kgd->qgjd", dscores.astype(jnp.float32), keys_all)
    key_part = jnp.einsum("gjqk,qgjd->kgd", dscores.astype(jnp.float32), heads_q)
    value_part = jnp.einsum("gjqk,qgjd->kgd", probs_b.astype(jnp.float32), grads_q)
    terms = jnp.stack([key_part.reshape(-1, KVH * HD), value_part.reshape(-1, KVH * HD)], axis=1)
    terms = terms.reshape(key_set.shape[0], rows, 2, KVH * HD)
    return (attended.reshape(rows, -1).astype(jnp.bfloat16), qgrad.reshape(rows, -1).astype(jnp.bfloat16), terms)


def reference(queries, keys, values, out_grad, rand_blocks, global_blocks):
    pair_blocks = jnp.stack([keys, values], axis=1).reshape(NB, BLOCK, 2, KW)
    query_blocks = queries.reshape(NB, BLOCK, QW)
    grad_blocks = out_grad.reshape(NB, BLOCK, QW)
    block_ids = jnp.arange(NB, dtype=jnp.int32)
    windows = (block_ids[:, None] + jnp.arange(-1, 2, dtype=jnp.int32)[None, :]) % NB
    key_lists = jnp.concatenate([windows.astype(jnp.int32), jnp.broadcast_to(global_blocks[None, :], (NB, GLOB)).astype(jnp.int32), rand_blocks.astype(jnp.int32)], axis=1)

    def per_block(inputs):
        query_block, grad_block, listing = inputs
        key_set = pair_blocks[listing]
        return attend((query_block, key_set, grad_block))

    out_blocks, qgrad_blocks, key_terms = lax.map(per_block, (query_blocks, grad_blocks, key_lists))
    window_terms = key_terms[:, :3].reshape(-1, BLOCK, 2, KW)
    total = jax.ops.segment_sum(window_terms, key_lists[:, :3].reshape(-1), num_segments=NB)
    rand_rounded = lax.optimization_barrier(key_terms[:, 3 + GLOB:].astype(jnp.bfloat16)).astype(jnp.float32)
    total = total + jax.ops.segment_sum(rand_rounded.reshape(-1, BLOCK, 2, KW), key_lists[:, 3 + GLOB:].reshape(-1), num_segments=NB)
    glob_sums = jnp.sum(key_terms[:, 3:3 + GLOB].reshape(N_SEQ, QB, GLOB, BLOCK, 2, KW), axis=1)
    glob_rounded = lax.optimization_barrier(glob_sums.astype(jnp.bfloat16)).astype(jnp.float32)
    glob_ids = jnp.broadcast_to(global_blocks[None, :], (N_SEQ, GLOB)).reshape(-1).astype(jnp.int32)
    total = total + jax.ops.segment_sum(glob_rounded.reshape(-1, BLOCK, 2, KW), glob_ids, num_segments=NB)
    out = out_blocks.reshape(TOKENS, QW)
    query_grad = qgrad_blocks.reshape(TOKENS, QW)
    key_grad = total[:, :, 0].reshape(TOKENS, KW).astype(jnp.bfloat16)
    value_grad = total[:, :, 1].reshape(TOKENS, KW).astype(jnp.bfloat16)
    return (out, query_grad, key_grad, value_grad)
```

```python
import math

import jax
import jax.numpy as jnp
from jax import lax
from jax.experimental import pallas as pl
from jax.experimental.pallas import tpu as pltpu
from jax.sharding import PartitionSpec as P

KVH = 2
HD = 128
BLOCK = 64
GLOB = 2
RAND = 3
GROUP = 4
QB = 4
NY = 8
NX = 4
FAR = RAND * QB + GLOB
KEYS = (3 + GLOB + RAND) * BLOCK
TOK = QB * BLOCK
SCALE = HD ** (-0.5)
LOG2E = math.log2(math.e)
F32 = jnp.float32
BF16 = jnp.bfloat16


def dot_nt(a, b):
    return lax.dot_general(a, b, (((1,), (1,)), ((), ())), preferred_element_type=F32)


def dot_nn(a, b):
    return lax.dot_general(a, b, (((1,), (0,)), ((), ())), preferred_element_type=F32)


def dot_tn(a, b):
    return lax.dot_general(a, b, (((0,), (0,)), ((), ())), preferred_element_type=F32)


HEAD_BUFFERS = (
    ("xg", (NX * QB, BLOCK, HD), BF16),
    ("yg", (NY * QB, BLOCK, HD), BF16),
    ("sk", (NY * NX, BLOCK, HD), BF16),
    ("rk", (NY * NX, BLOCK, HD), BF16),
    ("sv", (NX * NY, BLOCK, HD), BF16),
    ("rv", (NX * NY, BLOCK, HD), BF16),
    ("fk", (FAR, BLOCK, HD), BF16),
    ("fv", (FAR, BLOCK, HD), BF16),
    ("bsk", (NY * NX, BLOCK, HD), BF16),
    ("brk", (NY * NX, BLOCK, HD), BF16),
    ("bsv", (NX * NY, BLOCK, HD), BF16),
    ("brv", (NX * NY, BLOCK, HD), BF16),
    ("ak", (NX, TOK, HD), BF16),
    ("rak", (NX, TOK, HD), BF16),
    ("av", (NY, TOK, HD), F32),
    ("su", (4, TOK, HD), BF16),
    ("ru", (4, TOK, HD), BF16),
    ("sd", (4, TOK, HD), BF16),
    ("rd", (4, TOK, HD), BF16),
    ("kx", ((QB + 2) * BLOCK, HD), BF16),
    ("vx", ((QB + 2) * BLOCK, HD), BF16),
    ("wk", ((QB + 2) * BLOCK, HD), F32),
    ("wv", ((QB + 2) * BLOCK, HD), F32),
    ("gk", (GLOB * BLOCK, HD), F32),
    ("gv", (GLOB * BLOCK, HD), F32),
    ("rim_out", (2, 2, BLOCK, HD), BF16),
    ("rim_in", (2, 2, BLOCK, HD), BF16),
)
HEAD_COPIES = (
    ("xs", NX - 1), ("up", 4), ("down", 4), ("ks", NY - 1), ("vs", NX - 1),
    ("bks", NY - 1), ("bvs", NX - 1), ("axs", NX - 1), ("bup", 4), ("bdown", 4), ("rim", 4),
)


class Named:
    def __init__(self, names, refs):
        for name, ref in zip(names, refs, strict=True):
            setattr(self, name, ref)


def kernel(rb, gb, q_ref, k_ref, v_ref, g_ref, out_ref, qg_ref, kg_ref, vg_ref, *scratch):
    scratch = list(scratch)

    def take(n):
        got = scratch[:n]
        del scratch[:n]
        return got

    tk, tv, ent, halo, kc, vc = take(6)
    bufs = [Named([b[0] for b in HEAD_BUFFERS], take(len(HEAD_BUFFERS))) for _ in range(KVH)]
    halo_sems = take(2)
    sems = []
    for _ in range(KVH):
        refs = take(2 * len(HEAD_COPIES))
        sems.append(Named([c[0] for c in HEAD_COPIES], [(refs[2 * i], refs[2 * i + 1]) for i in range(len(HEAD_COPIES))]))

    me = lax.axis_index("seq")
    y, x = lax.div(me, NX), lax.rem(me, NX)

    def at(row, col):
        return lax.rem(row, NY) * NX + lax.rem(col, NX)

    col_peers = [at(y + d, x) for d in range(1, NY)]
    row_peers = [at(y, x + d) for d in range(1, NX)]
    up, down = at(y + 1, x), at(y + NY - 1, x)
    after = lax.rem(me + 1, NY * NX)
    before = lax.rem(me + NY * NX - 1, NY * NX)
    barrier = pltpu.get_barrier_semaphore()
    peers = col_peers + row_peers + [after, before]
    for peer in peers:
        pl.semaphore_signal(barrier, inc=1, device_id={"seq": peer}, device_id_type=pl.DeviceIdType.MESH)

    started = []

    def copy(src, dst, pair, i, peer):
        return pltpu.make_async_remote_copy(
            src_ref=src, dst_ref=dst, send_sem=pair[0].at[i], recv_sem=pair[1].at[i],
            device_id={"seq": peer}, device_id_type=pl.DeviceIdType.MESH,
        )

    def send(src, dst, pair, i, peer):
        c = copy(src, dst, pair, i, peer)
        c.start()
        started.append(c)

    def arrive(dst, pair, i):
        copy(dst, dst, pair, i, after).wait_recv()

    for h, b in enumerate(bufs):
        cols = slice(h * HD, (h + 1) * HD)
        b.xg[pl.ds(x * QB, QB)] = k_ref[:, cols].reshape(QB, BLOCK, HD)
        b.yg[pl.ds(y * QB, QB)] = v_ref[:, cols].reshape(QB, BLOCK, HD)
        b.kx[BLOCK : BLOCK + TOK] = k_ref[:, cols]
        b.vx[BLOCK : BLOCK + TOK] = v_ref[:, cols]

    pl.semaphore_wait(barrier, len(peers))

    for h, b in enumerate(bufs):
        cols = slice(h * HD, (h + 1) * HD)
        own = b.yg.at[pl.ds(y * QB, QB)]
        send(own, own, sems[h].up, 0, up)
        send(own, own, sems[h].down, 0, down)
        own = b.xg.at[pl.ds(x * QB, QB)]
        for i, peer in enumerate(row_peers):
            send(own, own, sems[h].xs, i, peer)
    send(k_ref.at[TOK - BLOCK : TOK], halo.at[0, 0], halo_sems, 0, after)
    send(v_ref.at[TOK - BLOCK : TOK], halo.at[0, 1], halo_sems, 1, after)
    send(k_ref.at[0:BLOCK], halo.at[1, 0], halo_sems, 2, before)
    send(v_ref.at[0:BLOCK], halo.at[1, 1], halo_sems, 3, before)

    def listed(device):
        ids = [rb[device * QB + e // RAND, e % RAND] for e in range(RAND * QB)]
        return ids + [gb[e] for e in range(GLOB)]

    def named(ids, owner, pick):
        found = jnp.int32(-1)
        for e, block in enumerate(ids):
            found = jnp.where((block >> 2) == owner, pick(e, block), found)
        return found

    @pl.loop(0, NY)
    def _(row):
        ids = listed(row * NX + x)
        for c in range(NX):
            tk[row * NX + c] = named(ids, y * NX + c, lambda e, block: block & 3)

    @pl.loop(0, NX)
    def _(col):
        ids = listed(y * NX + col)
        for r in range(NY):
            tv[col * NY + r] = named(ids, r * NX + x, lambda e, block: block & 3)

    mine = listed(me)

    @pl.loop(0, NY * NX)
    def _(owner):
        ent[owner] = jnp.maximum(named(mine, owner, lambda e, block: jnp.int32(e)), 0)

    half = TOK // 2
    for s in range(1, 4):
        for h, b in enumerate(bufs):
            lower, upper = lax.rem(y + NY - s, NY) * QB, lax.rem(y + s, NY) * QB
            n = QB if s < 3 else QB // 2
            arrive(b.yg.at[pl.ds(lower, QB)], sems[h].up, s - 1)
            part = b.yg.at[pl.ds(lower, n)]
            send(part, part, sems[h].up, s, up)
            arrive(b.yg.at[pl.ds(upper, QB)], sems[h].down, s - 1)
            part = b.yg.at[pl.ds(upper + QB - n, n)]
            send(part, part, sems[h].down, s, down)

    across = lax.rem(y + 4, NY)
    for h, b in enumerate(bufs):
        for i, d in enumerate(range(1, NX)):
            arrive(b.xg.at[pl.ds(lax.rem(x + NX - d, NX) * QB, QB)], sems[h].xs, i)

        @pl.loop(0, NY)
        def _(row):
            for c in range(NX):
                b.sk[row * NX + c] = b.xg[c * QB + jnp.maximum(tk[row * NX + c], 0)]

        for i, d in enumerate(range(1, NY)):
            row = lax.rem(y + d, NY)
            send(b.sk.at[pl.ds(row * NX, NX)], b.rk.at[pl.ds(y * NX, NX)], sems[h].ks, i, col_peers[i])
        b.rk[pl.ds(y * NX, NX)] = b.sk[pl.ds(y * NX, NX)]
        arrive(b.yg.at[pl.ds(across * QB, QB // 2)], sems[h].up, 3)
        arrive(b.yg.at[pl.ds(across * QB + QB // 2, QB // 2)], sems[h].down, 3)

        @pl.loop(0, NX)
        def _(col):
            for r in range(NY):
                b.sv[col * NY + r] = b.yg[r * QB + jnp.maximum(tv[col * NY + r], 0)]

        for i, d in enumerate(range(1, NX)):
            col = lax.rem(x + d, NX)
            send(b.sv.at[pl.ds(col * NY, NY)], b.rv.at[pl.ds(x * NY, NY)], sems[h].vs, i, row_peers[i])
        b.rv[pl.ds(x * NY, NY)] = b.sv[pl.ds(x * NY, NY)]

    for i in range(4):
        arrive(halo.at[i // 2, i % 2], halo_sems, i)
    for h, b in enumerate(bufs):
        cols = slice(h * HD, (h + 1) * HD)
        b.kx[0:BLOCK] = halo[0, 0, :, cols]
        b.vx[0:BLOCK] = halo[0, 1, :, cols]
        b.kx[BLOCK + TOK :] = halo[1, 0, :, cols]
        b.vx[BLOCK + TOK :] = halo[1, 1, :, cols]

    def compute(h):
        b = bufs[h]
        for ref in (b.wk, b.wv, b.gk, b.gv):
            ref[...] = jnp.zeros_like(ref)
        window, globe = 3 * BLOCK, GLOB * BLOCK
        for i in range(GLOB):
            owner = gb[i] >> 2
            kc[window + i * BLOCK : window + (i + 1) * BLOCK] = b.rk[owner]
            vc[window + i * BLOCK : window + (i + 1) * BLOCK] = b.rv[(owner & 3) * NY + (owner >> 2)]

        @pl.loop(0, QB)
        def _(j):
            rows = pl.ds(pl.multiple_of(j * BLOCK, BLOCK), BLOCK)
            span = pl.ds(pl.multiple_of(j * BLOCK, BLOCK), window)
            kc[0:window] = b.kx[span]
            vc[0:window] = b.vx[span]
            for i in range(RAND):
                owner = rb[me * QB + j, i] >> 2
                to = slice(window + globe + i * BLOCK, window + globe + (i + 1) * BLOCK)
                kc[to] = b.rk[owner]
                vc[to] = b.rv[(owner & 3) * NY + (owner >> 2)]
            base = h * GROUP * HD
            q = jnp.concatenate([q_ref[rows, base + i * HD : base + (i + 1) * HD] for i in range(GROUP)], axis=0)
            g = jnp.concatenate([g_ref[rows, base + i * HD : base + (i + 1) * HD] for i in range(GROUP)], axis=0)
            k, v = kc[...], vc[...]
            scores = dot_nt(q, k)
            peak = jnp.max(scores, axis=1, keepdims=True)
            expos = jnp.exp2((scores - peak) * (SCALE * LOG2E))
            probs = expos * (1.0 / jnp.sum(expos, axis=1, keepdims=True))
            probs_b = probs.astype(BF16)
            attended = dot_nn(probs_b, v)
            delta = jnp.sum(g.astype(F32) * attended, axis=1, keepdims=True)
            dprobs = dot_nt(g, v)
            dscores = (probs * (dprobs - delta)).astype(BF16)
            qgrad = dot_nn(dscores, k) * SCALE
            for i in range(GROUP):
                part = slice(i * BLOCK, (i + 1) * BLOCK)
                out_ref[rows, base + i * HD : base + (i + 1) * HD] = attended[part].astype(BF16)
                qg_ref[rows, base + i * HD : base + (i + 1) * HD] = qgrad[part].astype(BF16)
            key_part = dot_tn(dscores, q) * SCALE
            b.wk[span] += key_part[:window]
            b.gk[...] += key_part[window : window + globe]
            b.fk[pl.ds(j * RAND, RAND)] = key_part[window + globe :].astype(BF16).reshape(RAND, BLOCK, HD)
            value_part = dot_tn(probs_b, g)
            b.wv[span] += value_part[:window]
            b.gv[...] += value_part[window : window + globe]
            b.fv[pl.ds(j * RAND, RAND)] = value_part[window + globe :].astype(BF16).reshape(RAND, BLOCK, HD)

        b.fk[RAND * QB :] = b.gk[...].astype(BF16).reshape(GLOB, BLOCK, HD)
        b.fv[RAND * QB :] = b.gv[...].astype(BF16).reshape(GLOB, BLOCK, HD)

    def send_back(h):
        b = bufs[h]

        @pl.loop(0, NY * NX)
        def _(owner):
            b.bsk[owner] = b.fk[ent[owner]]

        for i, d in enumerate(range(1, NY)):
            row = lax.rem(y + d, NY)
            send(b.bsk.at[pl.ds(row * NX, NX)], b.brk.at[pl.ds(y * NX, NX)], sems[h].bks, i, col_peers[i])

        @pl.loop(0, NX)
        def _(col):
            for r in range(NY):
                b.bsv[col * NY + r] = b.fv[ent[r * NX + col]]

        for i, d in enumerate(range(1, NX)):
            col = lax.rem(x + d, NX)
            send(b.bsv.at[pl.ds(col * NY, NY)], b.brv.at[pl.ds(x * NY, NY)], sems[h].bvs, i, row_peers[i])
        b.brk[pl.ds(y * NX, NX)] = b.bsk[pl.ds(y * NX, NX)]
        b.brv[pl.ds(x * NY, NY)] = b.bsv[pl.ds(x * NY, NY)]
        b.rim_out[0, 0] = b.wk[(QB + 1) * BLOCK :].astype(BF16)
        b.rim_out[0, 1] = b.wv[(QB + 1) * BLOCK :].astype(BF16)
        b.rim_out[1, 0] = b.wk[0:BLOCK].astype(BF16)
        b.rim_out[1, 1] = b.wv[0:BLOCK].astype(BF16)
        for i in range(4):
            send(b.rim_out.at[i // 2, i % 2], b.rim_in.at[i // 2, i % 2], sems[h].rim, i, after if i < 2 else before)

    def reduce_values(h):
        b = bufs[h]
        for i, d in enumerate(range(1, NX)):
            arrive(b.brv.at[pl.ds(lax.rem(x + NX - d, NX) * NY, NY)], sems[h].bvs, i)

        @pl.loop(0, NY)
        def _(row):
            sums = [jnp.zeros((BLOCK, HD), F32) for _ in range(QB)]
            for c in range(NX):
                term = b.brv[c * NY + row].astype(F32)
                local = jnp.full((BLOCK, HD), tv[c * NY + row], jnp.int32)
                for i in range(QB):
                    sums[i] = sums[i] + jnp.where(local == i, term, 0.0)
            for i in range(QB):
                b.av[row, i * BLOCK : (i + 1) * BLOCK] = sums[i]

        b.su[0, 0:half] = b.av[across, 0:half].astype(BF16)
        b.sd[0, half:TOK] = b.av[across, half:TOK].astype(BF16)
        send(b.su.at[0, 0:half], b.ru.at[0, 0:half], sems[h].bup, 0, up)
        send(b.sd.at[0, half:TOK], b.rd.at[0, half:TOK], sems[h].bdown, 0, down)

    def reduce_keys(h):
        b = bufs[h]
        for i, d in enumerate(range(1, NY)):
            arrive(b.brk.at[pl.ds(lax.rem(y + NY - d, NY) * NX, NX)], sems[h].bks, i)

        @pl.loop(0, NX)
        def _(col):
            sums = [jnp.zeros((BLOCK, HD), F32) for _ in range(QB)]
            for r in range(NY):
                term = b.brk[r * NX + col].astype(F32)
                local = jnp.full((BLOCK, HD), tk[r * NX + col], jnp.int32)
                for i in range(QB):
                    sums[i] = sums[i] + jnp.where(local == i, term, 0.0)
            for i in range(QB):
                b.ak[col, i * BLOCK : (i + 1) * BLOCK] = sums[i].astype(BF16)

        for i, d in enumerate(range(1, NX)):
            send(b.ak.at[lax.rem(x + d, NX)], b.rak.at[x], sems[h].axs, i, row_peers[i])
        b.rak[x] = b.ak[x]

    def ring_step(h, s):
        b = bufs[h]
        rows = slice(0, half) if s == 1 else slice(0, TOK)
        arrive(b.ru.at[s - 1, rows], sems[h].bup, s - 1)
        ahead = lax.rem(y + 4 - s, NY)
        b.su[s, rows] = (b.av[ahead, rows] + b.ru[s - 1, rows].astype(F32)).astype(BF16)
        if s == 1:
            b.su[s, half:TOK] = b.av[ahead, half:TOK].astype(BF16)
        send(b.su.at[s], b.ru.at[s], sems[h].bup, s, up)
        rows = slice(half, TOK) if s == 1 else slice(0, TOK)
        arrive(b.rd.at[s - 1, rows], sems[h].bdown, s - 1)
        behind = lax.rem(y + 4 + s, NY)
        b.sd[s, rows] = (b.av[behind, rows] + b.rd[s - 1, rows].astype(F32)).astype(BF16)
        if s == 1:
            b.sd[s, 0:half] = b.av[behind, 0:half].astype(BF16)
        send(b.sd.at[s], b.rd.at[s], sems[h].bdown, s, down)

    def finish(h):
        b = bufs[h]
        cols = slice(h * HD, (h + 1) * HD)
        for i in range(4):
            arrive(b.rim_in.at[i // 2, i % 2], sems[h].rim, i)
        for i, d in enumerate(range(1, NX)):
            arrive(b.rak.at[lax.rem(x + NX - d, NX)], sems[h].axs, i)
        keys = b.wk[BLOCK : BLOCK + TOK]
        for c in range(NX):
            keys = keys + b.rak[c].astype(F32)
        last = slice(TOK - BLOCK, TOK)
        kg_ref[:, cols] = keys.astype(BF16)
        kg_ref[0:BLOCK, cols] = (keys[0:BLOCK] + b.rim_in[0, 0].astype(F32)).astype(BF16)
        kg_ref[last, cols] = (keys[last] + b.rim_in[1, 0].astype(F32)).astype(BF16)
        arrive(b.ru.at[3], sems[h].bup, 3)
        arrive(b.rd.at[3], sems[h].bdown, 3)
        vals = b.wv[BLOCK : BLOCK + TOK] + b.av[y] + b.ru[3].astype(F32) + b.rd[3].astype(F32)
        vg_ref[:, cols] = vals.astype(BF16)
        vg_ref[0:BLOCK, cols] = (vals[0:BLOCK] + b.rim_in[0, 1].astype(F32)).astype(BF16)
        vg_ref[last, cols] = (vals[last] + b.rim_in[1, 1].astype(F32)).astype(BF16)

    for h, b in enumerate(bufs):
        for i, d in enumerate(range(1, NY)):
            arrive(b.rk.at[pl.ds(lax.rem(y + NY - d, NY) * NX, NX)], sems[h].ks, i)
        for i, d in enumerate(range(1, NX)):
            arrive(b.rv.at[pl.ds(lax.rem(x + NX - d, NX) * NY, NY)], sems[h].vs, i)
        compute(h)
        send_back(h)
    for h in range(KVH):
        reduce_values(h)
        reduce_keys(h)
        for s in range(1, 4):
            ring_step(h, s)
    for h in range(KVH):
        finish(h)
    for c in started:
        c.wait_send()


def local(queries, keys, values, out_grad, rand_blocks, global_blocks):
    vmem = pl.BlockSpec(memory_space=pltpu.VMEM)
    smem = pl.BlockSpec(memory_space=pltpu.SMEM)
    sems = []
    for _ in range(KVH):
        for _, n in HEAD_COPIES:
            sems += [pltpu.SemaphoreType.DMA((n,))] * 2
    return pl.pallas_call(
        kernel,
        out_shape=(
            jax.ShapeDtypeStruct(queries.shape, BF16),
            jax.ShapeDtypeStruct(queries.shape, BF16),
            jax.ShapeDtypeStruct(keys.shape, BF16),
            jax.ShapeDtypeStruct(keys.shape, BF16),
        ),
        in_specs=[smem, smem, vmem, vmem, vmem, vmem],
        out_specs=(vmem, vmem, vmem, vmem),
        scratch_shapes=[
            pltpu.SMEM((NY * NX,), jnp.int32),
            pltpu.SMEM((NX * NY,), jnp.int32),
            pltpu.SMEM((NY * NX,), jnp.int32),
            pltpu.VMEM((2, 2, BLOCK, KVH * HD), BF16),
            pltpu.VMEM((KEYS, HD), BF16),
            pltpu.VMEM((KEYS, HD), BF16),
            *[pltpu.VMEM(shape, dtype) for _ in range(KVH) for _, shape, dtype in HEAD_BUFFERS],
            pltpu.SemaphoreType.DMA((4,)),
            pltpu.SemaphoreType.DMA((4,)),
            *sems,
        ],
        compiler_params=pltpu.CompilerParams(collective_id=0, has_side_effects=True),
        name="genome_attention",
    )(rand_blocks, global_blocks, queries, keys, values, out_grad)


def solution(mesh):
    tokens, parts = P(("dp", "seq"), None), P("dp", None)
    return jax.shard_map(
        local,
        mesh=mesh,
        in_specs=(tokens, tokens, tokens, tokens, parts, P("dp")),
        out_specs=(tokens, tokens, tokens, tokens),
        check_vma=False,
    )
```

```python
import math

import jax
import jax.numpy as jnp
from jax import lax
from jax.experimental import pallas as pl
from jax.experimental.pallas import tpu as pltpu
from jax.sharding import PartitionSpec as P

KVH = 2
HD = 128
BLOCK = 64
GLOB = 2
RAND = 3
GROUP = 4
QB = 4
NY = 8
NX = 4
FAR = RAND * QB + GLOB
KEYS = (3 + GLOB + RAND) * BLOCK
TOK = QB * BLOCK
SCALE = HD ** (-0.5)
LOG2E = math.log2(math.e)
F32 = jnp.float32
BF16 = jnp.bfloat16


def dot_nt(a, b):
    return lax.dot_general(a, b, (((1,), (1,)), ((), ())), preferred_element_type=F32)


def dot_nn(a, b):
    return lax.dot_general(a, b, (((1,), (0,)), ((), ())), preferred_element_type=F32)


def dot_tn(a, b):
    return lax.dot_general(a, b, (((0,), (0,)), ((), ())), preferred_element_type=F32)


HEAD_BUFFERS = (
    ("xg", (NX * QB, BLOCK, HD), BF16),
    ("yg", (NY * QB, BLOCK, HD), BF16),
    ("sk", (NY * NX, BLOCK, HD), BF16),
    ("rk", (NY * NX, BLOCK, HD), BF16),
    ("sv", (NX * NY, BLOCK, HD), BF16),
    ("rv", (NX * NY, BLOCK, HD), BF16),
    ("fk", (FAR, BLOCK, HD), BF16),
    ("fv", (FAR, BLOCK, HD), BF16),
    ("bsk", (NY * NX, BLOCK, HD), BF16),
    ("brk", (NY * NX, BLOCK, HD), BF16),
    ("bsv", (NX * NY, BLOCK, HD), BF16),
    ("brv", (NX * NY, BLOCK, HD), BF16),
    ("ak", (NX, TOK, HD), BF16),
    ("rak", (NX, TOK, HD), BF16),
    ("av", (NY, TOK, HD), F32),
    ("su", (4, TOK, HD), BF16),
    ("ru", (4, TOK, HD), BF16),
    ("sd", (4, TOK, HD), BF16),
    ("rd", (4, TOK, HD), BF16),
    ("kx", ((QB + 2) * BLOCK, HD), BF16),
    ("vx", ((QB + 2) * BLOCK, HD), BF16),
    ("wk", ((QB + 2) * BLOCK, HD), F32),
    ("wv", ((QB + 2) * BLOCK, HD), F32),
    ("gk", (GLOB * BLOCK, HD), F32),
    ("gv", (GLOB * BLOCK, HD), F32),
    ("rim_out", (2, 2, BLOCK, HD), BF16),
    ("rim_in", (2, 2, BLOCK, HD), BF16),
)
HEAD_COPIES = (
    ("xs", NX - 1), ("up", 4), ("down", 4), ("ks", NY - 1), ("vs", NX - 1),
    ("bks", NY - 1), ("bvs", NX - 1), ("axs", NX - 1), ("bup", 4), ("bdown", 4), ("rim", 4),
)


class Named:
    def __init__(self, names, refs):
        for name, ref in zip(names, refs, strict=True):
            setattr(self, name, ref)


def kernel(rb, gb, q_hbm, k_ref, v_ref, g_hbm, out_ref, qg_ref, kg_ref, vg_ref, *scratch):
    scratch = list(scratch)

    def take(n):
        got = scratch[:n]
        del scratch[:n]
        return got

    tk, tv, ent, halo, kc, vc, q_ref, g_ref, load_sems = take(9)
    bufs = [Named([b[0] for b in HEAD_BUFFERS], take(len(HEAD_BUFFERS))) for _ in range(KVH)]
    halo_sems = take(2)
    sems = []
    for _ in range(KVH):
        refs = take(2 * len(HEAD_COPIES))
        sems.append(Named([c[0] for c in HEAD_COPIES], [(refs[2 * i], refs[2 * i + 1]) for i in range(len(HEAD_COPIES))]))

    me = lax.axis_index("seq")
    y, x = lax.div(me, NX), lax.rem(me, NX)

    def at(row, col):
        return lax.rem(row, NY) * NX + lax.rem(col, NX)

    col_peers = [at(y + d, x) for d in range(1, NY)]
    row_peers = [at(y, x + d) for d in range(1, NX)]
    up, down = at(y + 1, x), at(y + NY - 1, x)
    after = lax.rem(me + 1, NY * NX)
    before = lax.rem(me + NY * NX - 1, NY * NX)
    barrier = pltpu.get_barrier_semaphore()
    peers = col_peers + row_peers + [after, before]
    for peer in peers:
        pl.semaphore_signal(barrier, inc=1, device_id={"seq": peer}, device_id_type=pl.DeviceIdType.MESH)

    loads = [pltpu.make_async_copy(q_hbm, q_ref, load_sems.at[0]), pltpu.make_async_copy(g_hbm, g_ref, load_sems.at[1])]
    for c in loads:
        c.start()
    started = []

    def copy(src, dst, pair, i, peer):
        return pltpu.make_async_remote_copy(
            src_ref=src, dst_ref=dst, send_sem=pair[0].at[i], recv_sem=pair[1].at[i],
            device_id={"seq": peer}, device_id_type=pl.DeviceIdType.MESH,
        )

    def send(src, dst, pair, i, peer):
        c = copy(src, dst, pair, i, peer)
        c.start()
        started.append(c)

    def arrive(dst, pair, i):
        copy(dst, dst, pair, i, after).wait_recv()

    for h, b in enumerate(bufs):
        cols = slice(h * HD, (h + 1) * HD)
        b.xg[pl.ds(x * QB, QB)] = k_ref[:, cols].reshape(QB, BLOCK, HD)
        b.yg[pl.ds(y * QB, QB)] = v_ref[:, cols].reshape(QB, BLOCK, HD)
        b.kx[BLOCK : BLOCK + TOK] = k_ref[:, cols]
        b.vx[BLOCK : BLOCK + TOK] = v_ref[:, cols]

    pl.semaphore_wait(barrier, len(peers))

    for h, b in enumerate(bufs):
        cols = slice(h * HD, (h + 1) * HD)
        own = b.yg.at[pl.ds(y * QB, QB)]
        send(own, own, sems[h].up, 0, up)
        send(own, own, sems[h].down, 0, down)
        own = b.xg.at[pl.ds(x * QB, QB)]
        for i, peer in enumerate(row_peers):
            send(own, own, sems[h].xs, i, peer)
    send(k_ref.at[TOK - BLOCK : TOK], halo.at[0, 0], halo_sems, 0, after)
    send(v_ref.at[TOK - BLOCK : TOK], halo.at[0, 1], halo_sems, 1, after)
    send(k_ref.at[0:BLOCK], halo.at[1, 0], halo_sems, 2, before)
    send(v_ref.at[0:BLOCK], halo.at[1, 1], halo_sems, 3, before)

    def listed(device):
        ids = [rb[e % RAND, device * QB + e // RAND] for e in range(RAND * QB)]
        return ids + [gb[e] for e in range(GLOB)]

    def named(ids, owner, pick):
        found = jnp.int32(-1)
        for e, block in enumerate(ids):
            found = jnp.where((block >> 2) == owner, pick(e, block), found)
        return found

    @pl.loop(0, NY)
    def _(row):
        ids = listed(row * NX + x)
        for c in range(NX):
            tk[row * NX + c] = named(ids, y * NX + c, lambda e, block: block & 3)

    @pl.loop(0, NX)
    def _(col):
        ids = listed(y * NX + col)
        for r in range(NY):
            tv[col * NY + r] = named(ids, r * NX + x, lambda e, block: block & 3)

    mine = listed(me)

    @pl.loop(0, NY * NX)
    def _(owner):
        ent[owner] = jnp.maximum(named(mine, owner, lambda e, block: jnp.int32(e)), 0)

    half = TOK // 2
    for s in range(1, 4):
        for h, b in enumerate(bufs):
            lower, upper = lax.rem(y + NY - s, NY) * QB, lax.rem(y + s, NY) * QB
            n = QB if s < 3 else QB // 2
            arrive(b.yg.at[pl.ds(lower, QB)], sems[h].up, s - 1)
            part = b.yg.at[pl.ds(lower, n)]
            send(part, part, sems[h].up, s, up)
            arrive(b.yg.at[pl.ds(upper, QB)], sems[h].down, s - 1)
            part = b.yg.at[pl.ds(upper + QB - n, n)]
            send(part, part, sems[h].down, s, down)

    across = lax.rem(y + 4, NY)
    for h, b in enumerate(bufs):
        for i, d in enumerate(range(1, NX)):
            arrive(b.xg.at[pl.ds(lax.rem(x + NX - d, NX) * QB, QB)], sems[h].xs, i)

        @pl.loop(0, NY)
        def _(row):
            for c in range(NX):
                b.sk[row * NX + c] = b.xg[c * QB + jnp.maximum(tk[row * NX + c], 0)]

        for i, d in enumerate(range(1, NY)):
            row = lax.rem(y + d, NY)
            send(b.sk.at[pl.ds(row * NX, NX)], b.rk.at[pl.ds(y * NX, NX)], sems[h].ks, i, col_peers[i])
        b.rk[pl.ds(y * NX, NX)] = b.sk[pl.ds(y * NX, NX)]
        arrive(b.yg.at[pl.ds(across * QB, QB // 2)], sems[h].up, 3)
        arrive(b.yg.at[pl.ds(across * QB + QB // 2, QB // 2)], sems[h].down, 3)

        @pl.loop(0, NX)
        def _(col):
            for r in range(NY):
                b.sv[col * NY + r] = b.yg[r * QB + jnp.maximum(tv[col * NY + r], 0)]

        for i, d in enumerate(range(1, NX)):
            col = lax.rem(x + d, NX)
            send(b.sv.at[pl.ds(col * NY, NY)], b.rv.at[pl.ds(x * NY, NY)], sems[h].vs, i, row_peers[i])
        b.rv[pl.ds(x * NY, NY)] = b.sv[pl.ds(x * NY, NY)]

    for i in range(4):
        arrive(halo.at[i // 2, i % 2], halo_sems, i)
    for h, b in enumerate(bufs):
        cols = slice(h * HD, (h + 1) * HD)
        b.kx[0:BLOCK] = halo[0, 0, :, cols]
        b.vx[0:BLOCK] = halo[0, 1, :, cols]
        b.kx[BLOCK + TOK :] = halo[1, 0, :, cols]
        b.vx[BLOCK + TOK :] = halo[1, 1, :, cols]

    for c in loads:
        c.wait()

    def compute(h):
        b = bufs[h]
        for ref in (b.wk, b.wv, b.gk, b.gv):
            ref[...] = jnp.zeros_like(ref)
        window, globe = 3 * BLOCK, GLOB * BLOCK
        for i in range(GLOB):
            owner = gb[i] >> 2
            kc[window + i * BLOCK : window + (i + 1) * BLOCK] = b.rk[owner]
            vc[window + i * BLOCK : window + (i + 1) * BLOCK] = b.rv[(owner & 3) * NY + (owner >> 2)]

        @pl.loop(0, QB)
        def _(j):
            rows = pl.ds(pl.multiple_of(j * BLOCK, BLOCK), BLOCK)
            span = pl.ds(pl.multiple_of(j * BLOCK, BLOCK), window)
            kc[0:window] = b.kx[span]
            vc[0:window] = b.vx[span]
            for i in range(RAND):
                owner = rb[i, me * QB + j] >> 2
                to = slice(window + globe + i * BLOCK, window + globe + (i + 1) * BLOCK)
                kc[to] = b.rk[owner]
                vc[to] = b.rv[(owner & 3) * NY + (owner >> 2)]
            base = h * GROUP * HD
            q = jnp.concatenate([q_ref[rows, base + i * HD : base + (i + 1) * HD] for i in range(GROUP)], axis=0)
            g = jnp.concatenate([g_ref[rows, base + i * HD : base + (i + 1) * HD] for i in range(GROUP)], axis=0)
            k, v = kc[...], vc[...]
            scores = dot_nt(q, k)
            peak = jnp.max(scores, axis=1, keepdims=True)
            expos = jnp.exp2((scores - peak) * (SCALE * LOG2E))
            probs = expos * (1.0 / jnp.sum(expos, axis=1, keepdims=True))
            probs_b = probs.astype(BF16)
            attended = dot_nn(probs_b, v)
            delta = jnp.sum(g.astype(F32) * attended, axis=1, keepdims=True)
            dprobs = dot_nt(g, v)
            dscores = (probs * (dprobs - delta)).astype(BF16)
            qgrad = dot_nn(dscores, k) * SCALE
            for i in range(GROUP):
                part = slice(i * BLOCK, (i + 1) * BLOCK)
                out_ref[rows, base + i * HD : base + (i + 1) * HD] = attended[part].astype(BF16)
                qg_ref[rows, base + i * HD : base + (i + 1) * HD] = qgrad[part].astype(BF16)
            key_part = dot_tn(dscores, q) * SCALE
            b.wk[span] += key_part[:window]
            b.gk[...] += key_part[window : window + globe]
            b.fk[pl.ds(j * RAND, RAND)] = key_part[window + globe :].astype(BF16).reshape(RAND, BLOCK, HD)
            value_part = dot_tn(probs_b, g)
            b.wv[span] += value_part[:window]
            b.gv[...] += value_part[window : window + globe]
            b.fv[pl.ds(j * RAND, RAND)] = value_part[window + globe :].astype(BF16).reshape(RAND, BLOCK, HD)

        b.fk[RAND * QB :] = b.gk[...].astype(BF16).reshape(GLOB, BLOCK, HD)
        b.fv[RAND * QB :] = b.gv[...].astype(BF16).reshape(GLOB, BLOCK, HD)

    def send_back(h):
        b = bufs[h]

        @pl.loop(0, NY * NX)
        def _(owner):
            b.bsk[owner] = b.fk[ent[owner]]

        for i, d in enumerate(range(1, NY)):
            row = lax.rem(y + d, NY)
            send(b.bsk.at[pl.ds(row * NX, NX)], b.brk.at[pl.ds(y * NX, NX)], sems[h].bks, i, col_peers[i])

        @pl.loop(0, NX)
        def _(col):
            for r in range(NY):
                b.bsv[col * NY + r] = b.fv[ent[r * NX + col]]

        for i, d in enumerate(range(1, NX)):
            col = lax.rem(x + d, NX)
            send(b.bsv.at[pl.ds(col * NY, NY)], b.brv.at[pl.ds(x * NY, NY)], sems[h].bvs, i, row_peers[i])
        b.brk[pl.ds(y * NX, NX)] = b.bsk[pl.ds(y * NX, NX)]
        b.brv[pl.ds(x * NY, NY)] = b.bsv[pl.ds(x * NY, NY)]
        b.rim_out[0, 0] = b.wk[(QB + 1) * BLOCK :].astype(BF16)
        b.rim_out[0, 1] = b.wv[(QB + 1) * BLOCK :].astype(BF16)
        b.rim_out[1, 0] = b.wk[0:BLOCK].astype(BF16)
        b.rim_out[1, 1] = b.wv[0:BLOCK].astype(BF16)
        for i in range(4):
            send(b.rim_out.at[i // 2, i % 2], b.rim_in.at[i // 2, i % 2], sems[h].rim, i, after if i < 2 else before)

    def reduce_values(h):
        b = bufs[h]
        for i, d in enumerate(range(1, NX)):
            arrive(b.brv.at[pl.ds(lax.rem(x + NX - d, NX) * NY, NY)], sems[h].bvs, i)

        @pl.loop(0, NY)
        def _(row):
            sums = [jnp.zeros((BLOCK, HD), F32) for _ in range(QB)]
            for c in range(NX):
                term = b.brv[c * NY + row].astype(F32)
                local = jnp.full((BLOCK, HD), tv[c * NY + row], jnp.int32)
                for i in range(QB):
                    sums[i] = sums[i] + jnp.where(local == i, term, 0.0)
            for i in range(QB):
                b.av[row, i * BLOCK : (i + 1) * BLOCK] = sums[i]

        b.su[0, 0:half] = b.av[across, 0:half].astype(BF16)
        b.sd[0, half:TOK] = b.av[across, half:TOK].astype(BF16)
        send(b.su.at[0, 0:half], b.ru.at[0, 0:half], sems[h].bup, 0, up)
        send(b.sd.at[0, half:TOK], b.rd.at[0, half:TOK], sems[h].bdown, 0, down)

    def reduce_keys(h):
        b = bufs[h]
        for i, d in enumerate(range(1, NY)):
            arrive(b.brk.at[pl.ds(lax.rem(y + NY - d, NY) * NX, NX)], sems[h].bks, i)

        @pl.loop(0, NX)
        def _(col):
            sums = [jnp.zeros((BLOCK, HD), F32) for _ in range(QB)]
            for r in range(NY):
                term = b.brk[r * NX + col].astype(F32)
                local = jnp.full((BLOCK, HD), tk[r * NX + col], jnp.int32)
                for i in range(QB):
                    sums[i] = sums[i] + jnp.where(local == i, term, 0.0)
            for i in range(QB):
                b.ak[col, i * BLOCK : (i + 1) * BLOCK] = sums[i].astype(BF16)

        for i, d in enumerate(range(1, NX)):
            send(b.ak.at[lax.rem(x + d, NX)], b.rak.at[x], sems[h].axs, i, row_peers[i])
        b.rak[x] = b.ak[x]

    def ring_step(h, s):
        b = bufs[h]
        rows = slice(0, half) if s == 1 else slice(0, TOK)
        arrive(b.ru.at[s - 1, rows], sems[h].bup, s - 1)
        ahead = lax.rem(y + 4 - s, NY)
        b.su[s, rows] = (b.av[ahead, rows] + b.ru[s - 1, rows].astype(F32)).astype(BF16)
        if s == 1:
            b.su[s, half:TOK] = b.av[ahead, half:TOK].astype(BF16)
        send(b.su.at[s], b.ru.at[s], sems[h].bup, s, up)
        rows = slice(half, TOK) if s == 1 else slice(0, TOK)
        arrive(b.rd.at[s - 1, rows], sems[h].bdown, s - 1)
        behind = lax.rem(y + 4 + s, NY)
        b.sd[s, rows] = (b.av[behind, rows] + b.rd[s - 1, rows].astype(F32)).astype(BF16)
        if s == 1:
            b.sd[s, 0:half] = b.av[behind, 0:half].astype(BF16)
        send(b.sd.at[s], b.rd.at[s], sems[h].bdown, s, down)

    def finish(h):
        b = bufs[h]
        cols = slice(h * HD, (h + 1) * HD)
        for i in range(4):
            arrive(b.rim_in.at[i // 2, i % 2], sems[h].rim, i)
        for i, d in enumerate(range(1, NX)):
            arrive(b.rak.at[lax.rem(x + NX - d, NX)], sems[h].axs, i)
        keys = b.wk[BLOCK : BLOCK + TOK]
        for c in range(NX):
            keys = keys + b.rak[c].astype(F32)
        last = slice(TOK - BLOCK, TOK)
        kg_ref[:, cols] = keys.astype(BF16)
        kg_ref[0:BLOCK, cols] = (keys[0:BLOCK] + b.rim_in[0, 0].astype(F32)).astype(BF16)
        kg_ref[last, cols] = (keys[last] + b.rim_in[1, 0].astype(F32)).astype(BF16)
        arrive(b.ru.at[3], sems[h].bup, 3)
        arrive(b.rd.at[3], sems[h].bdown, 3)
        vals = b.wv[BLOCK : BLOCK + TOK] + b.av[y] + b.ru[3].astype(F32) + b.rd[3].astype(F32)
        vg_ref[:, cols] = vals.astype(BF16)
        vg_ref[0:BLOCK, cols] = (vals[0:BLOCK] + b.rim_in[0, 1].astype(F32)).astype(BF16)
        vg_ref[last, cols] = (vals[last] + b.rim_in[1, 1].astype(F32)).astype(BF16)

    for h, b in enumerate(bufs):
        for i, d in enumerate(range(1, NY)):
            arrive(b.rk.at[pl.ds(lax.rem(y + NY - d, NY) * NX, NX)], sems[h].ks, i)
        for i, d in enumerate(range(1, NX)):
            arrive(b.rv.at[pl.ds(lax.rem(x + NX - d, NX) * NY, NY)], sems[h].vs, i)
        compute(h)
        send_back(h)
    reduce_values(0)
    reduce_values(1)
    for s in range(1, 4):
        for h in range(KVH):
            ring_step(h, s)
        if s <= KVH:
            reduce_keys(s - 1)
    for h in range(KVH):
        finish(h)
    for c in started:
        c.wait_send()


def store(*refs):
    copies = [pltpu.make_async_copy(refs[i], refs[4 + i], refs[8].at[i]) for i in range(4)]
    for c in copies:
        c.start()
    for c in copies:
        c.wait()


def local(queries, keys, values, out_grad, rand_blocks, global_blocks):
    vmem = pl.BlockSpec(memory_space=pltpu.VMEM)
    smem = pl.BlockSpec(memory_space=pltpu.SMEM)
    hbm = pl.BlockSpec(memory_space=pl.ANY)
    sems = []
    for _ in range(KVH):
        for _, n in HEAD_COPIES:
            sems += [pltpu.SemaphoreType.DMA((n,))] * 2
    shapes = [queries.shape, queries.shape, keys.shape, keys.shape]
    held = pl.pallas_call(
        kernel,
        out_shape=tuple(pltpu.VMEM(shape, BF16) for shape in shapes),
        in_specs=[smem, smem, hbm, vmem, vmem, hbm],
        out_specs=(vmem, vmem, vmem, vmem),
        scratch_shapes=[
            pltpu.SMEM((NY * NX,), jnp.int32),
            pltpu.SMEM((NX * NY,), jnp.int32),
            pltpu.SMEM((NY * NX,), jnp.int32),
            pltpu.VMEM((2, 2, BLOCK, KVH * HD), BF16),
            pltpu.VMEM((KEYS, HD), BF16),
            pltpu.VMEM((KEYS, HD), BF16),
            pltpu.VMEM(queries.shape, BF16),
            pltpu.VMEM(queries.shape, BF16),
            pltpu.SemaphoreType.DMA((2,)),
            *[pltpu.VMEM(shape, dtype) for _ in range(KVH) for _, shape, dtype in HEAD_BUFFERS],
            pltpu.SemaphoreType.DMA((4,)),
            pltpu.SemaphoreType.DMA((4,)),
            *sems,
        ],
        compiler_params=pltpu.CompilerParams(collective_id=0, has_side_effects=True),
        name="genome_attention",
    )(rand_blocks.T, global_blocks, queries, keys, values, out_grad)
    return pl.pallas_call(
        store,
        out_shape=tuple(jax.ShapeDtypeStruct(shape, BF16) for shape in shapes),
        in_specs=[vmem] * 4,
        out_specs=(hbm,) * 4,
        scratch_shapes=[pltpu.SemaphoreType.DMA((4,))],
        name="store_outputs",
    )(*[pltpu.with_memory_space_constraint(array, pltpu.VMEM) for array in held])


def solution(mesh):
    tokens, parts = P(("dp", "seq"), None), P("dp", None)
    return jax.shard_map(
        local,
        mesh=mesh,
        in_specs=(tokens, tokens, tokens, tokens, parts, P("dp")),
        out_specs=(tokens, tokens, tokens, tokens),
        check_vma=False,
    )
```

```python
import math

import jax
import jax.numpy as jnp
from jax import lax
from jax.experimental import pallas as pl
from jax.experimental.pallas import tpu as pltpu
from jax.sharding import PartitionSpec as P

KVH = 2
HD = 128
BLOCK = 64
GLOB = 2
RAND = 3
GROUP = 4
QB = 4
NY = 8
NX = 4
NEAR = 5
ROW_ORDER = (4, 3, 5, 2, 6, 1, 7)
FAR = RAND * QB + GLOB
KEYS = (3 + GLOB + RAND) * BLOCK
TOK = QB * BLOCK
SCALE = HD ** (-0.5)
LOG2E = math.log2(math.e)
F32 = jnp.float32
BF16 = jnp.bfloat16


def dot_nt(a, b):
    return lax.dot_general(a, b, (((1,), (1,)), ((), ())), preferred_element_type=F32)


def dot_nn(a, b):
    return lax.dot_general(a, b, (((1,), (0,)), ((), ())), preferred_element_type=F32)


def dot_tn(a, b):
    return lax.dot_general(a, b, (((0,), (0,)), ((), ())), preferred_element_type=F32)


HEAD_BUFFERS = (
    ("xg", (NX * QB, BLOCK, HD), BF16),
    ("yn", (NEAR * QB, BLOCK, HD), BF16),
    ("yf", ((NY - NEAR) * QB, BLOCK, HD), BF16),
    ("sk", (NY * NX, BLOCK, HD), BF16),
    ("rk", (NY * NX, BLOCK, HD), BF16),
    ("sv", (NX * NY, BLOCK, HD), BF16),
    ("rv", (NX * NY, BLOCK, HD), BF16),
    ("fk", (FAR, BLOCK, HD), BF16),
    ("fv", (FAR, BLOCK, HD), BF16),
    ("bsk", (NY * NX, BLOCK, HD), BF16),
    ("brk", (NY * NX, BLOCK, HD), BF16),
    ("bsv", (NX * NY, BLOCK, HD), BF16),
    ("brv", (NX * NY, BLOCK, HD), BF16),
    ("ak", (NX, TOK, HD), BF16),
    ("rak", (NX, TOK, HD), BF16),
    ("av", (NY, TOK, HD), F32),
    ("su", (4, TOK, HD), BF16),
    ("ru", (4, TOK, HD), BF16),
    ("sd", (4, TOK, HD), BF16),
    ("rd", (4, TOK, HD), BF16),
    ("kx", ((QB + 2) * BLOCK, HD), BF16),
    ("vx", ((QB + 2) * BLOCK, HD), BF16),
    ("wk", ((QB + 2) * BLOCK, HD), F32),
    ("wv", ((QB + 2) * BLOCK, HD), F32),
    ("gk", (GLOB * BLOCK, HD), F32),
    ("gv", (GLOB * BLOCK, HD), F32),
    ("rim_out", (2, 2, BLOCK, HD), BF16),
    ("rim_in", (2, 2, BLOCK, HD), BF16),
)
HEAD_COPIES = (
    ("xs", NX - 1), ("up", 4), ("down", 4), ("ks", NY - 1), ("vn", NX - 1), ("vf", NX - 1),
    ("bks", NY - 1), ("bvn", NX - 1), ("bvf", NX - 1), ("axs", NX - 1), ("bup", 4), ("bdown", 4), ("rim", 4),
)


class Named:
    def __init__(self, names, refs):
        for name, ref in zip(names, refs, strict=True):
            setattr(self, name, ref)


def kernel(rb, gb, q_hbm, k_ref, v_ref, g_hbm, out_ref, qg_ref, kg_ref, vg_ref, *scratch):
    scratch = list(scratch)

    def take(n):
        got = scratch[:n]
        del scratch[:n]
        return got

    tk, tv, ent, halo, kc, vc, q_ref, g_ref, load_sems = take(9)
    bufs = [Named([b[0] for b in HEAD_BUFFERS], take(len(HEAD_BUFFERS))) for _ in range(KVH)]
    halo_sems = take(2)
    sems = []
    for _ in range(KVH):
        refs = take(2 * len(HEAD_COPIES))
        sems.append(Named([c[0] for c in HEAD_COPIES], [(refs[2 * i], refs[2 * i + 1]) for i in range(len(HEAD_COPIES))]))

    me = lax.axis_index("seq")
    y, x = lax.div(me, NX), lax.rem(me, NX)

    def at(row, col):
        return lax.rem(row, NY) * NX + lax.rem(col, NX)

    col_peers = [at(y + d, x) for d in range(1, NY)]
    row_peers = [at(y, x + d) for d in range(1, NX)]
    up, down = at(y + 1, x), at(y + NY - 1, x)
    after = lax.rem(me + 1, NY * NX)
    before = lax.rem(me + NY * NX - 1, NY * NX)
    barrier = pltpu.get_barrier_semaphore()
    peers = col_peers + row_peers + [after, before]
    for peer in peers:
        pl.semaphore_signal(barrier, inc=1, device_id={"seq": peer}, device_id_type=pl.DeviceIdType.MESH)

    loads = [pltpu.make_async_copy(q_hbm, q_ref, load_sems.at[0]), pltpu.make_async_copy(g_hbm, g_ref, load_sems.at[1])]
    for c in loads:
        c.start()
    started = []

    def copy(src, dst, pair, i, peer):
        return pltpu.make_async_remote_copy(
            src_ref=src, dst_ref=dst, send_sem=pair[0].at[i], recv_sem=pair[1].at[i],
            device_id={"seq": peer}, device_id_type=pl.DeviceIdType.MESH,
        )

    def send(src, dst, pair, i, peer):
        c = copy(src, dst, pair, i, peer)
        c.start()
        started.append(c)

    def arrive(dst, pair, i):
        copy(dst, dst, pair, i, after).wait_recv()

    for h, b in enumerate(bufs):
        cols = slice(h * HD, (h + 1) * HD)
        b.xg[pl.ds(x * QB, QB)] = k_ref[:, cols].reshape(QB, BLOCK, HD)
        b.yn[2 * QB : 3 * QB] = v_ref[:, cols].reshape(QB, BLOCK, HD)
        b.kx[BLOCK : BLOCK + TOK] = k_ref[:, cols]
        b.vx[BLOCK : BLOCK + TOK] = v_ref[:, cols]

    pl.semaphore_wait(barrier, len(peers))

    def held(b, i, first=0, n=QB):
        ref, i = (b.yn, i) if i < NEAR else (b.yf, i - NEAR)
        return ref.at[i * QB + first : i * QB + first + n]

    def ring_out(h, s):
        b = bufs[h]
        n = QB if s < 3 else QB // 2
        send(held(b, (2 - s) % NY, 0, n), held(b, (1 - s) % NY, 0, n), sems[h].up, s, up)
        send(held(b, 2 + s, QB - n, n), held(b, 3 + s, QB - n, n), sems[h].down, s, down)

    def ring_in(h, s):
        b = bufs[h]
        n = QB if s < 3 else QB // 2
        arrive(held(b, (1 - s) % NY, 0, n), sems[h].up, s)
        arrive(held(b, 3 + s, QB - n, n), sems[h].down, s)

    for h in range(KVH):
        ring_out(h, 0)
    for h, b in enumerate(bufs):
        own = b.xg.at[pl.ds(x * QB, QB)]
        for i, peer in enumerate(row_peers):
            send(own, own, sems[h].xs, i, peer)

    def listed(device):
        ids = [rb[e % RAND, device * QB + e // RAND] for e in range(RAND * QB)]
        return ids + [gb[e] for e in range(GLOB)]

    def named(ids, owner, pick):
        found = jnp.int32(-1)
        for e, block in enumerate(ids):
            found = jnp.where((block >> 2) == owner, pick(e, block), found)
        return found

    @pl.loop(0, NY)
    def _(row):
        ids = listed(row * NX + x)
        for c in range(NX):
            tk[row * NX + c] = named(ids, y * NX + c, lambda e, block: block & 3)

    @pl.loop(0, NX)
    def _(col):
        ids = listed(y * NX + col)
        for i in range(NY):
            owner = lax.rem(y + i + NY - 2, NY) * NX + x
            tv[col * NY + i] = named(ids, owner, lambda e, block: block & 3)

    mine = listed(me)

    @pl.loop(0, NY * NX)
    def _(owner):
        ent[owner] = jnp.maximum(named(mine, owner, lambda e, block: jnp.int32(e)), 0)

    half = TOK // 2

    def send_keys(h):
        b = bufs[h]
        for i, d in enumerate(range(1, NX)):
            arrive(b.xg.at[pl.ds(lax.rem(x + NX - d, NX) * QB, QB)], sems[h].xs, i)

        @pl.loop(0, NY)
        def _(row):
            for c in range(NX):
                b.sk[row * NX + c] = b.xg[c * QB + jnp.maximum(tk[row * NX + c], 0)]

        for d in ROW_ORDER:
            row = lax.rem(y + d, NY)
            send(b.sk.at[pl.ds(row * NX, NX)], b.rk.at[pl.ds(y * NX, NX)], sems[h].ks, d - 1, col_peers[d - 1])
        b.rk[pl.ds(y * NX, NX)] = b.sk[pl.ds(y * NX, NX)]

    def send_values(h, near):
        b = bufs[h]
        first, n = (0, NEAR) if near else (NEAR, NY - NEAR)
        ref = b.yn if near else b.yf

        @pl.loop(0, NX)
        def _(col):
            for i in range(n):
                b.sv[col * NY + first + i] = ref[i * QB + jnp.maximum(tv[col * NY + first + i], 0)]

        for i, d in enumerate(range(1, NX)):
            col = lax.rem(x + d, NX)
            send(
                b.sv.at[pl.ds(col * NY + first, n)], b.rv.at[pl.ds(x * NY + first, n)],
                sems[h].vn if near else sems[h].vf, i, row_peers[i],
            )
        b.rv[pl.ds(x * NY + first, n)] = b.sv[pl.ds(x * NY + first, n)]

    for s in range(2):
        for h in range(KVH):
            ring_in(h, s)
            ring_out(h, s + 1)
    send_values(0, True)
    send(k_ref.at[TOK - BLOCK : TOK], halo.at[0, 0], halo_sems, 0, after)
    send(v_ref.at[TOK - BLOCK : TOK], halo.at[0, 1], halo_sems, 1, after)
    send(k_ref.at[0:BLOCK], halo.at[1, 0], halo_sems, 2, before)
    send(v_ref.at[0:BLOCK], halo.at[1, 1], halo_sems, 3, before)
    for h in range(KVH):
        ring_in(h, 2)
        ring_out(h, 3)
    send_keys(0)
    ring_in(0, 3)
    send_values(0, False)
    send_values(1, True)
    ring_in(1, 3)
    send_values(1, False)
    send_keys(1)

    for i in range(4):
        arrive(halo.at[i // 2, i % 2], halo_sems, i)
    for h, b in enumerate(bufs):
        cols = slice(h * HD, (h + 1) * HD)
        b.kx[0:BLOCK] = halo[0, 0, :, cols]
        b.vx[0:BLOCK] = halo[0, 1, :, cols]
        b.kx[BLOCK + TOK :] = halo[1, 0, :, cols]
        b.vx[BLOCK + TOK :] = halo[1, 1, :, cols]

    for c in loads:
        c.wait()

    def compute(h):
        b = bufs[h]
        for ref in (b.wk, b.wv, b.gk, b.gv):
            ref[...] = jnp.zeros_like(ref)
        window, globe = 3 * BLOCK, GLOB * BLOCK
        for i in range(GLOB):
            owner = gb[i] >> 2
            kc[window + i * BLOCK : window + (i + 1) * BLOCK] = b.rk[owner]
            vc[window + i * BLOCK : window + (i + 1) * BLOCK] = b.rv[(owner & 3) * NY + (((owner >> 2) + NY + 2 - y) & 7)]

        @pl.loop(0, QB)
        def _(j):
            rows = pl.ds(pl.multiple_of(j * BLOCK, BLOCK), BLOCK)
            span = pl.ds(pl.multiple_of(j * BLOCK, BLOCK), window)
            kc[0:window] = b.kx[span]
            vc[0:window] = b.vx[span]
            for i in range(RAND):
                owner = rb[i, me * QB + j] >> 2
                to = slice(window + globe + i * BLOCK, window + globe + (i + 1) * BLOCK)
                kc[to] = b.rk[owner]
                vc[to] = b.rv[(owner & 3) * NY + (((owner >> 2) + NY + 2 - y) & 7)]
            base = h * GROUP * HD
            q = jnp.concatenate([q_ref[rows, base + i * HD : base + (i + 1) * HD] for i in range(GROUP)], axis=0)
            g = jnp.concatenate([g_ref[rows, base + i * HD : base + (i + 1) * HD] for i in range(GROUP)], axis=0)
            k, v = kc[...], vc[...]
            scores = dot_nt(q, k)
            peak = jnp.max(scores, axis=1, keepdims=True)
            expos = jnp.exp2((scores - peak) * (SCALE * LOG2E))
            probs = expos * (1.0 / jnp.sum(expos, axis=1, keepdims=True))
            probs_b = probs.astype(BF16)
            attended = dot_nn(probs_b, v)
            delta = jnp.sum(g.astype(F32) * attended, axis=1, keepdims=True)
            dprobs = dot_nt(g, v)
            dscores = (probs * (dprobs - delta)).astype(BF16)
            qgrad = dot_nn(dscores, k) * SCALE
            for i in range(GROUP):
                part = slice(i * BLOCK, (i + 1) * BLOCK)
                out_ref[rows, base + i * HD : base + (i + 1) * HD] = attended[part].astype(BF16)
                qg_ref[rows, base + i * HD : base + (i + 1) * HD] = qgrad[part].astype(BF16)
            key_part = dot_tn(dscores, q) * SCALE
            b.wk[span] += key_part[:window]
            b.gk[...] += key_part[window : window + globe]
            b.fk[pl.ds(j * RAND, RAND)] = key_part[window + globe :].astype(BF16).reshape(RAND, BLOCK, HD)
            value_part = dot_tn(probs_b, g)
            b.wv[span] += value_part[:window]
            b.gv[...] += value_part[window : window + globe]
            b.fv[pl.ds(j * RAND, RAND)] = value_part[window + globe :].astype(BF16).reshape(RAND, BLOCK, HD)

        b.fk[RAND * QB :] = b.gk[...].astype(BF16).reshape(GLOB, BLOCK, HD)
        b.fv[RAND * QB :] = b.gv[...].astype(BF16).reshape(GLOB, BLOCK, HD)

    def pack_back(h):
        b = bufs[h]

        @pl.loop(0, NX)
        def _(col):
            for i in range(NY):
                b.bsv[col * NY + i] = b.fv[ent[lax.rem(y + i + NY - 2, NY) * NX + col]]

        @pl.loop(0, NY * NX)
        def _(owner):
            b.bsk[owner] = b.fk[ent[owner]]

    def values_back(h):
        b = bufs[h]
        for near in (False, True):
            first, n = (0, NEAR) if near else (NEAR, NY - NEAR)
            for i, d in enumerate(range(1, NX)):
                col = lax.rem(x + d, NX)
                send(
                    b.bsv.at[pl.ds(col * NY + first, n)], b.brv.at[pl.ds(x * NY + first, n)],
                    sems[h].bvn if near else sems[h].bvf, i, row_peers[i],
                )
        b.brv[pl.ds(x * NY, NY)] = b.bsv[pl.ds(x * NY, NY)]

    def keys_back(h, distances):
        b = bufs[h]
        for d in distances:
            row = lax.rem(y + d, NY)
            send(b.bsk.at[pl.ds(row * NX, NX)], b.brk.at[pl.ds(y * NX, NX)], sems[h].bks, d - 1, col_peers[d - 1])
        if distances[-1] == ROW_ORDER[-1]:
            b.brk[pl.ds(y * NX, NX)] = b.bsk[pl.ds(y * NX, NX)]

    def rims_back(h):
        b = bufs[h]
        b.rim_out[0, 0] = b.wk[(QB + 1) * BLOCK :].astype(BF16)
        b.rim_out[0, 1] = b.wv[(QB + 1) * BLOCK :].astype(BF16)
        b.rim_out[1, 0] = b.wk[0:BLOCK].astype(BF16)
        b.rim_out[1, 1] = b.wv[0:BLOCK].astype(BF16)
        for i in range(4):
            send(b.rim_out.at[i // 2, i % 2], b.rim_in.at[i // 2, i % 2], sems[h].rim, i, after if i < 2 else before)

    def reduce_values(h, near):
        b = bufs[h]
        first, n = (0, NEAR) if near else (NEAR, NY - NEAR)
        for i, d in enumerate(range(1, NX)):
            arrive(
                b.brv.at[pl.ds(lax.rem(x + NX - d, NX) * NY + first, n)],
                sems[h].bvn if near else sems[h].bvf, i,
            )

        @pl.loop(first, first + n)
        def _(row):
            sums = [jnp.zeros((BLOCK, HD), F32) for _ in range(QB)]
            for c in range(NX):
                term = b.brv[c * NY + row].astype(F32)
                local = jnp.full((BLOCK, HD), tv[c * NY + row], jnp.int32)
                for i in range(QB):
                    sums[i] = sums[i] + jnp.where(local == i, term, 0.0)
            for i in range(QB):
                b.av[row, i * BLOCK : (i + 1) * BLOCK] = sums[i]

        if not near:
            b.su[0, 0:half] = b.av[6, 0:half].astype(BF16)
            b.sd[0, half:TOK] = b.av[6, half:TOK].astype(BF16)
            send(b.su.at[0, 0:half], b.ru.at[0, 0:half], sems[h].bup, 0, up)
            send(b.sd.at[0, half:TOK], b.rd.at[0, half:TOK], sems[h].bdown, 0, down)

    def reduce_keys(h):
        b = bufs[h]
        for i, d in enumerate(range(1, NY)):
            arrive(b.brk.at[pl.ds(lax.rem(y + NY - d, NY) * NX, NX)], sems[h].bks, i)

        @pl.loop(0, NX)
        def _(col):
            sums = [jnp.zeros((BLOCK, HD), F32) for _ in range(QB)]
            for r in range(NY):
                term = b.brk[r * NX + col].astype(F32)
                local = jnp.full((BLOCK, HD), tk[r * NX + col], jnp.int32)
                for i in range(QB):
                    sums[i] = sums[i] + jnp.where(local == i, term, 0.0)
            for i in range(QB):
                b.ak[col, i * BLOCK : (i + 1) * BLOCK] = sums[i].astype(BF16)

        for i, d in enumerate(range(1, NX)):
            send(b.ak.at[lax.rem(x + d, NX)], b.rak.at[x], sems[h].axs, i, row_peers[i])
        b.rak[x] = b.ak[x]

    def ring_step(h, s):
        b = bufs[h]
        rows = slice(0, half) if s == 1 else slice(0, TOK)
        arrive(b.ru.at[s - 1, rows], sems[h].bup, s - 1)
        ahead, behind = 6 - s, (6 + s) % NY
        b.su[s, rows] = (b.av[ahead, rows] + b.ru[s - 1, rows].astype(F32)).astype(BF16)
        if s == 1:
            b.su[s, half:TOK] = b.av[ahead, half:TOK].astype(BF16)
        send(b.su.at[s], b.ru.at[s], sems[h].bup, s, up)
        rows = slice(half, TOK) if s == 1 else slice(0, TOK)
        arrive(b.rd.at[s - 1, rows], sems[h].bdown, s - 1)
        b.sd[s, rows] = (b.av[behind, rows] + b.rd[s - 1, rows].astype(F32)).astype(BF16)
        if s == 1:
            b.sd[s, 0:half] = b.av[behind, 0:half].astype(BF16)
        send(b.sd.at[s], b.rd.at[s], sems[h].bdown, s, down)

    def finish(h):
        b = bufs[h]
        cols = slice(h * HD, (h + 1) * HD)
        for i in range(4):
            arrive(b.rim_in.at[i // 2, i % 2], sems[h].rim, i)
        for i, d in enumerate(range(1, NX)):
            arrive(b.rak.at[lax.rem(x + NX - d, NX)], sems[h].axs, i)
        keys = b.wk[BLOCK : BLOCK + TOK]
        for c in range(NX):
            keys = keys + b.rak[c].astype(F32)
        last = slice(TOK - BLOCK, TOK)
        kg_ref[:, cols] = keys.astype(BF16)
        kg_ref[0:BLOCK, cols] = (keys[0:BLOCK] + b.rim_in[0, 0].astype(F32)).astype(BF16)
        kg_ref[last, cols] = (keys[last] + b.rim_in[1, 0].astype(F32)).astype(BF16)
        arrive(b.ru.at[3], sems[h].bup, 3)
        arrive(b.rd.at[3], sems[h].bdown, 3)
        vals = b.wv[BLOCK : BLOCK + TOK] + b.av[2] + b.ru[3].astype(F32) + b.rd[3].astype(F32)
        vg_ref[:, cols] = vals.astype(BF16)
        vg_ref[0:BLOCK, cols] = (vals[0:BLOCK] + b.rim_in[0, 1].astype(F32)).astype(BF16)
        vg_ref[last, cols] = (vals[last] + b.rim_in[1, 1].astype(F32)).astype(BF16)

    for h, b in enumerate(bufs):
        for i, d in enumerate(range(1, NY)):
            arrive(b.rk.at[pl.ds(lax.rem(y + NY - d, NY) * NX, NX)], sems[h].ks, i)
        for i, d in enumerate(range(1, NX)):
            col = lax.rem(x + NX - d, NX) * NY
            arrive(b.rv.at[pl.ds(col, NEAR)], sems[h].vn, i)
            arrive(b.rv.at[pl.ds(col + NEAR, NY - NEAR)], sems[h].vf, i)
        compute(h)
        pack_back(h)
        values_back(h)
        keys_back(h, ROW_ORDER if h == 0 else ROW_ORDER[:2])
    keys_back(1, ROW_ORDER[2:])
    for h in range(KVH):
        rims_back(h)
    reduce_values(0, False)
    reduce_values(1, False)
    reduce_values(0, True)
    ring_step(0, 1)
    ring_step(1, 1)
    reduce_keys(0)
    reduce_values(1, True)
    ring_step(0, 2)
    ring_step(1, 2)
    reduce_keys(1)
    ring_step(0, 3)
    ring_step(1, 3)
    for h in range(KVH):
        finish(h)
    for c in started:
        c.wait_send()


def store(*refs):
    copies = [pltpu.make_async_copy(refs[i], refs[4 + i], refs[8].at[i]) for i in range(4)]
    for c in copies:
        c.start()
    for c in copies:
        c.wait()


def local(queries, keys, values, out_grad, rand_blocks, global_blocks):
    vmem = pl.BlockSpec(memory_space=pltpu.VMEM)
    smem = pl.BlockSpec(memory_space=pltpu.SMEM)
    hbm = pl.BlockSpec(memory_space=pl.ANY)
    sems = []
    for _ in range(KVH):
        for _, n in HEAD_COPIES:
            sems += [pltpu.SemaphoreType.DMA((n,))] * 2
    shapes = [queries.shape, queries.shape, keys.shape, keys.shape]
    held = pl.pallas_call(
        kernel,
        out_shape=tuple(pltpu.VMEM(shape, BF16) for shape in shapes),
        in_specs=[smem, smem, hbm, vmem, vmem, hbm],
        out_specs=(vmem, vmem, vmem, vmem),
        scratch_shapes=[
            pltpu.SMEM((NY * NX,), jnp.int32),
            pltpu.SMEM((NX * NY,), jnp.int32),
            pltpu.SMEM((NY * NX,), jnp.int32),
            pltpu.VMEM((2, 2, BLOCK, KVH * HD), BF16),
            pltpu.VMEM((KEYS, HD), BF16),
            pltpu.VMEM((KEYS, HD), BF16),
            pltpu.VMEM(queries.shape, BF16),
            pltpu.VMEM(queries.shape, BF16),
            pltpu.SemaphoreType.DMA((2,)),
            *[pltpu.VMEM(shape, dtype) for _ in range(KVH) for _, shape, dtype in HEAD_BUFFERS],
            pltpu.SemaphoreType.DMA((4,)),
            pltpu.SemaphoreType.DMA((4,)),
            *sems,
        ],
        compiler_params=pltpu.CompilerParams(collective_id=0, has_side_effects=True),
        name="genome_attention",
    )(rand_blocks.T, global_blocks, queries, keys, values, out_grad)
    return pl.pallas_call(
        store,
        out_shape=tuple(jax.ShapeDtypeStruct(shape, BF16) for shape in shapes),
        in_specs=[vmem] * 4,
        out_specs=(hbm,) * 4,
        scratch_shapes=[pltpu.SemaphoreType.DMA((4,))],
        name="store_outputs",
    )(*[pltpu.with_memory_space_constraint(array, pltpu.VMEM) for array in held])


def solution(mesh):
    tokens, parts = P(("dp", "seq"), None), P("dp", None)
    return jax.shard_map(
        local,
        mesh=mesh,
        in_specs=(tokens, tokens, tokens, tokens, parts, P("dp")),
        out_specs=(tokens, tokens, tokens, tokens),
        check_vma=False,
    )
```

```python
import math

import jax
import jax.numpy as jnp
from jax import lax
from jax.experimental import pallas as pl
from jax.experimental.pallas import tpu as pltpu
from jax.sharding import PartitionSpec as P

KVH = 2
HD = 128
BLOCK = 64
GLOB = 2
RAND = 3
GROUP = 4
QB = 4
NY = 8
NX = 4
NEAR = 5
ROW_ORDER = (4, 3, 5, 2, 6, 1, 7)
FAR = RAND * QB + GLOB
KEYS = (3 + GLOB + RAND) * BLOCK
TOK = QB * BLOCK
SCALE = HD ** (-0.5)
LOG2E = math.log2(math.e)
F32 = jnp.float32
BF16 = jnp.bfloat16


def dot_nt(a, b):
    return lax.dot_general(a, b, (((1,), (1,)), ((), ())), preferred_element_type=F32)


def dot_nn(a, b):
    return lax.dot_general(a, b, (((1,), (0,)), ((), ())), preferred_element_type=F32)


def dot_tn(a, b):
    return lax.dot_general(a, b, (((0,), (0,)), ((), ())), preferred_element_type=F32)


HEAD_BUFFERS = (
    ("xg", (NX * QB, BLOCK, HD), BF16),
    ("yn", (NEAR * QB, BLOCK, HD), BF16),
    ("yf", ((NY - NEAR) * QB, BLOCK, HD), BF16),
    ("sk", (NY * NX, BLOCK, HD), BF16),
    ("rk", (NY * NX, BLOCK, HD), BF16),
    ("sv", (NX * NY, BLOCK, HD), BF16),
    ("rv", (NX * NY, BLOCK, HD), BF16),
    ("fk", (FAR, BLOCK, HD), BF16),
    ("fv", (FAR, BLOCK, HD), BF16),
    ("bsk", (NY * NX, BLOCK, HD), BF16),
    ("brk", (NY * NX, BLOCK, HD), BF16),
    ("bsv", (NX * NY, BLOCK, HD), BF16),
    ("brv", (NX * NY, BLOCK, HD), BF16),
    ("ak", (NX, TOK, HD), BF16),
    ("rak", (NX, TOK, HD), BF16),
    ("av", (NY, TOK, HD), F32),
    ("su", (4, TOK, HD), BF16),
    ("ru", (4, TOK, HD), BF16),
    ("sd", (4, TOK, HD), BF16),
    ("rd", (4, TOK, HD), BF16),
    ("kx", ((QB + 2) * BLOCK, HD), BF16),
    ("vx", ((QB + 2) * BLOCK, HD), BF16),
    ("wk", ((QB + 2) * BLOCK, HD), F32),
    ("wv", ((QB + 2) * BLOCK, HD), F32),
    ("gk", (GLOB * BLOCK, HD), F32),
    ("gv", (GLOB * BLOCK, HD), F32),
    ("rim_out", (2, 2, BLOCK, HD), BF16),
    ("rim_in", (2, 2, BLOCK, HD), BF16),
)
HEAD_COPIES = (
    ("xs", NX - 1), ("up", 4), ("down", 4), ("ks", NY - 1), ("vn", NX - 1), ("vf", NX - 1),
    ("bks", NY - 1), ("bvn", NX - 1), ("bvf", NX - 1), ("axs", NX - 1), ("bup", 4), ("bdown", 4), ("rim", 4),
)


class Named:
    def __init__(self, names, refs):
        for name, ref in zip(names, refs, strict=True):
            setattr(self, name, ref)


def kernel(rb, gb, q_hbm, k_ref, v_ref, g_hbm, out_ref, qg_ref, kg_ref, vg_ref, *scratch):
    scratch = list(scratch)

    def take(n):
        got = scratch[:n]
        del scratch[:n]
        return got

    tk, tv, ent, halo, kc, vc, q_ref, g_ref, load_sems = take(9)
    bufs = [Named([b[0] for b in HEAD_BUFFERS], take(len(HEAD_BUFFERS))) for _ in range(KVH)]
    halo_sems = take(2)
    sems = []
    for _ in range(KVH):
        refs = take(2 * len(HEAD_COPIES))
        sems.append(Named([c[0] for c in HEAD_COPIES], [(refs[2 * i], refs[2 * i + 1]) for i in range(len(HEAD_COPIES))]))

    me = lax.axis_index("seq")
    y, x = lax.div(me, NX), lax.rem(me, NX)

    def at(row, col):
        return lax.rem(row, NY) * NX + lax.rem(col, NX)

    col_peers = [at(y + d, x) for d in range(1, NY)]
    row_peers = [at(y, x + d) for d in range(1, NX)]
    up, down = at(y + 1, x), at(y + NY - 1, x)
    after = lax.rem(me + 1, NY * NX)
    before = lax.rem(me + NY * NX - 1, NY * NX)
    barrier = pltpu.get_barrier_semaphore()
    peers = col_peers + row_peers + [after, before]
    for peer in peers:
        pl.semaphore_signal(barrier, inc=1, device_id={"seq": peer}, device_id_type=pl.DeviceIdType.MESH)

    loads = [pltpu.make_async_copy(q_hbm, q_ref, load_sems.at[0]), pltpu.make_async_copy(g_hbm, g_ref, load_sems.at[1])]
    for c in loads:
        c.start()
    started = []

    def copy(src, dst, pair, i, peer):
        return pltpu.make_async_remote_copy(
            src_ref=src, dst_ref=dst, send_sem=pair[0].at[i], recv_sem=pair[1].at[i],
            device_id={"seq": peer}, device_id_type=pl.DeviceIdType.MESH,
        )

    def send(src, dst, pair, i, peer):
        c = copy(src, dst, pair, i, peer)
        c.start()
        started.append(c)

    def arrive(dst, pair, i):
        copy(dst, dst, pair, i, after).wait_recv()

    for h, b in enumerate(bufs):
        cols = slice(h * HD, (h + 1) * HD)
        b.xg[pl.ds(x * QB, QB)] = k_ref[:, cols].reshape(QB, BLOCK, HD)
        b.yn[2 * QB : 3 * QB] = v_ref[:, cols].reshape(QB, BLOCK, HD)
        b.kx[BLOCK : BLOCK + TOK] = k_ref[:, cols]
        b.vx[BLOCK : BLOCK + TOK] = v_ref[:, cols]

    pl.semaphore_wait(barrier, len(peers))

    def held(b, i, first=0, n=QB):
        ref, i = (b.yn, i) if i < NEAR else (b.yf, i - NEAR)
        return ref.at[i * QB + first : i * QB + first + n]

    def ring_out(h, s):
        b = bufs[h]
        n = QB if s < 3 else QB // 2
        send(held(b, (2 - s) % NY, 0, n), held(b, (1 - s) % NY, 0, n), sems[h].up, s, up)
        send(held(b, 2 + s, QB - n, n), held(b, 3 + s, QB - n, n), sems[h].down, s, down)

    def ring_in(h, s):
        b = bufs[h]
        n = QB if s < 3 else QB // 2
        arrive(held(b, (1 - s) % NY, 0, n), sems[h].up, s)
        arrive(held(b, 3 + s, QB - n, n), sems[h].down, s)

    send(k_ref.at[TOK - BLOCK : TOK], halo.at[0, 0], halo_sems, 0, after)
    send(v_ref.at[TOK - BLOCK : TOK], halo.at[0, 1], halo_sems, 1, after)
    send(k_ref.at[0:BLOCK], halo.at[1, 0], halo_sems, 2, before)
    send(v_ref.at[0:BLOCK], halo.at[1, 1], halo_sems, 3, before)
    for h in range(KVH):
        ring_out(h, 0)
    for h, b in enumerate(bufs):
        own = b.xg.at[pl.ds(x * QB, QB)]
        for i, peer in enumerate(row_peers):
            send(own, own, sems[h].xs, i, peer)

    def listed(device):
        ids = [rb[e % RAND, device * QB + e // RAND] for e in range(RAND * QB)]
        return ids + [gb[e] for e in range(GLOB)]

    def named(ids, owner, pick):
        found = jnp.int32(-1)
        for e, block in enumerate(ids):
            found = jnp.where((block >> 2) == owner, pick(e, block), found)
        return found

    @pl.loop(0, NY)
    def _(row):
        ids = listed(row * NX + x)
        for c in range(NX):
            tk[row * NX + c] = named(ids, y * NX + c, lambda e, block: block & 3)

    @pl.loop(0, NX)
    def _(col):
        ids = listed(y * NX + col)
        for i in range(NY):
            owner = lax.rem(y + i + NY - 2, NY) * NX + x
            tv[col * NY + i] = named(ids, owner, lambda e, block: block & 3)

    mine = listed(me)

    @pl.loop(0, NY * NX)
    def _(owner):
        ent[owner] = jnp.maximum(named(mine, owner, lambda e, block: jnp.int32(e)), 0)

    half = TOK // 2

    def send_keys(h):
        b = bufs[h]
        for i, d in enumerate(range(1, NX)):
            arrive(b.xg.at[pl.ds(lax.rem(x + NX - d, NX) * QB, QB)], sems[h].xs, i)

        @pl.loop(0, NY)
        def _(row):
            for c in range(NX):
                b.sk[row * NX + c] = b.xg[c * QB + jnp.maximum(tk[row * NX + c], 0)]

        for d in ROW_ORDER:
            row = lax.rem(y + d, NY)
            send(b.sk.at[pl.ds(row * NX, NX)], b.rk.at[pl.ds(y * NX, NX)], sems[h].ks, d - 1, col_peers[d - 1])
        b.rk[pl.ds(y * NX, NX)] = b.sk[pl.ds(y * NX, NX)]

    def send_values(h, near):
        b = bufs[h]
        first, n = (0, NEAR) if near else (NEAR, NY - NEAR)
        ref = b.yn if near else b.yf

        @pl.loop(0, NX)
        def _(col):
            for i in range(n):
                b.sv[col * NY + first + i] = ref[i * QB + jnp.maximum(tv[col * NY + first + i], 0)]

        for i, d in enumerate(range(1, NX)):
            col = lax.rem(x + d, NX)
            send(
                b.sv.at[pl.ds(col * NY + first, n)], b.rv.at[pl.ds(x * NY + first, n)],
                sems[h].vn if near else sems[h].vf, i, row_peers[i],
            )
        b.rv[pl.ds(x * NY + first, n)] = b.sv[pl.ds(x * NY + first, n)]

    for s in range(2):
        for h in range(KVH):
            ring_in(h, s)
            ring_out(h, s + 1)
    send_values(0, True)
    for h in range(KVH):
        ring_in(h, 2)
        ring_out(h, 3)
    send_keys(0)
    ring_in(0, 3)
    send_values(0, False)
    send_values(1, True)
    ring_in(1, 3)
    send_values(1, False)
    send_keys(1)

    for i in range(4):
        arrive(halo.at[i // 2, i % 2], halo_sems, i)
    for h, b in enumerate(bufs):
        cols = slice(h * HD, (h + 1) * HD)
        b.kx[0:BLOCK] = halo[0, 0, :, cols]
        b.vx[0:BLOCK] = halo[0, 1, :, cols]
        b.kx[BLOCK + TOK :] = halo[1, 0, :, cols]
        b.vx[BLOCK + TOK :] = halo[1, 1, :, cols]

    for c in loads:
        c.wait()

    def compute(h):
        b = bufs[h]
        for ref in (b.wk, b.wv, b.gk, b.gv):
            ref[...] = jnp.zeros_like(ref)
        window, globe = 3 * BLOCK, GLOB * BLOCK
        for i in range(GLOB):
            owner = gb[i] >> 2
            kc[window + i * BLOCK : window + (i + 1) * BLOCK] = b.rk[owner]
            vc[window + i * BLOCK : window + (i + 1) * BLOCK] = b.rv[(owner & 3) * NY + (((owner >> 2) + NY + 2 - y) & 7)]

        @pl.loop(0, QB)
        def _(j):
            rows = pl.ds(pl.multiple_of(j * BLOCK, BLOCK), BLOCK)
            span = pl.ds(pl.multiple_of(j * BLOCK, BLOCK), window)
            kc[0:window] = b.kx[span]
            vc[0:window] = b.vx[span]
            for i in range(RAND):
                owner = rb[i, me * QB + j] >> 2
                to = slice(window + globe + i * BLOCK, window + globe + (i + 1) * BLOCK)
                kc[to] = b.rk[owner]
                vc[to] = b.rv[(owner & 3) * NY + (((owner >> 2) + NY + 2 - y) & 7)]
            base = h * GROUP * HD
            q = jnp.concatenate([q_ref[rows, base + i * HD : base + (i + 1) * HD] for i in range(GROUP)], axis=0)
            g = jnp.concatenate([g_ref[rows, base + i * HD : base + (i + 1) * HD] for i in range(GROUP)], axis=0)
            k, v = kc[...], vc[...]
            scores = dot_nt(q, k)
            peak = jnp.max(scores, axis=1, keepdims=True)
            expos = jnp.exp2((scores - peak) * (SCALE * LOG2E))
            probs = expos * (1.0 / jnp.sum(expos, axis=1, keepdims=True))
            probs_b = probs.astype(BF16)
            attended = dot_nn(probs_b, v)
            delta = jnp.sum(g.astype(F32) * attended, axis=1, keepdims=True)
            dprobs = dot_nt(g, v)
            dscores = (probs * (dprobs - delta)).astype(BF16)
            qgrad = dot_nn(dscores, k) * SCALE
            for i in range(GROUP):
                part = slice(i * BLOCK, (i + 1) * BLOCK)
                out_ref[rows, base + i * HD : base + (i + 1) * HD] = attended[part].astype(BF16)
                qg_ref[rows, base + i * HD : base + (i + 1) * HD] = qgrad[part].astype(BF16)
            key_part = dot_tn(dscores, q) * SCALE
            b.wk[span] += key_part[:window]
            b.gk[...] += key_part[window : window + globe]
            b.fk[pl.ds(j * RAND, RAND)] = key_part[window + globe :].astype(BF16).reshape(RAND, BLOCK, HD)
            value_part = dot_tn(probs_b, g)
            b.wv[span] += value_part[:window]
            b.gv[...] += value_part[window : window + globe]
            b.fv[pl.ds(j * RAND, RAND)] = value_part[window + globe :].astype(BF16).reshape(RAND, BLOCK, HD)

        b.fk[RAND * QB :] = b.gk[...].astype(BF16).reshape(GLOB, BLOCK, HD)
        b.fv[RAND * QB :] = b.gv[...].astype(BF16).reshape(GLOB, BLOCK, HD)

    def pack_back(h):
        b = bufs[h]

        @pl.loop(0, NX)
        def _(col):
            for i in range(NY):
                b.bsv[col * NY + i] = b.fv[ent[lax.rem(y + i + NY - 2, NY) * NX + col]]

        @pl.loop(0, NY * NX)
        def _(owner):
            b.bsk[owner] = b.fk[ent[owner]]

    def values_back(h):
        b = bufs[h]
        for near in (False, True):
            first, n = (0, NEAR) if near else (NEAR, NY - NEAR)
            for i, d in enumerate(range(1, NX)):
                col = lax.rem(x + d, NX)
                send(
                    b.bsv.at[pl.ds(col * NY + first, n)], b.brv.at[pl.ds(x * NY + first, n)],
                    sems[h].bvn if near else sems[h].bvf, i, row_peers[i],
                )
        b.brv[pl.ds(x * NY, NY)] = b.bsv[pl.ds(x * NY, NY)]

    def keys_back(h, distances):
        b = bufs[h]
        for d in distances:
            row = lax.rem(y + d, NY)
            send(b.bsk.at[pl.ds(row * NX, NX)], b.brk.at[pl.ds(y * NX, NX)], sems[h].bks, d - 1, col_peers[d - 1])
        if distances[-1] == ROW_ORDER[-1]:
            b.brk[pl.ds(y * NX, NX)] = b.bsk[pl.ds(y * NX, NX)]

    def rims_back(h):
        b = bufs[h]
        b.rim_out[0, 0] = b.wk[(QB + 1) * BLOCK :].astype(BF16)
        b.rim_out[0, 1] = b.wv[(QB + 1) * BLOCK :].astype(BF16)
        b.rim_out[1, 0] = b.wk[0:BLOCK].astype(BF16)
        b.rim_out[1, 1] = b.wv[0:BLOCK].astype(BF16)
        for i in range(4):
            send(b.rim_out.at[i // 2, i % 2], b.rim_in.at[i // 2, i % 2], sems[h].rim, i, after if i < 2 else before)

    def reduce_values(h, near):
        b = bufs[h]
        first, n = (0, NEAR) if near else (NEAR, NY - NEAR)
        for i, d in enumerate(range(1, NX)):
            arrive(
                b.brv.at[pl.ds(lax.rem(x + NX - d, NX) * NY + first, n)],
                sems[h].bvn if near else sems[h].bvf, i,
            )

        @pl.loop(first, first + n)
        def _(row):
            sums = [jnp.zeros((BLOCK, HD), F32) for _ in range(QB)]
            for c in range(NX):
                term = b.brv[c * NY + row].astype(F32)
                local = jnp.full((BLOCK, HD), tv[c * NY + row], jnp.int32)
                for i in range(QB):
                    sums[i] = sums[i] + jnp.where(local == i, term, 0.0)
            for i in range(QB):
                b.av[row, i * BLOCK : (i + 1) * BLOCK] = sums[i]

        if not near:
            b.su[0, 0:half] = b.av[6, 0:half].astype(BF16)
            b.sd[0, half:TOK] = b.av[6, half:TOK].astype(BF16)
            send(b.su.at[0, 0:half], b.ru.at[0, 0:half], sems[h].bup, 0, up)
            send(b.sd.at[0, half:TOK], b.rd.at[0, half:TOK], sems[h].bdown, 0, down)

    def reduce_keys(h):
        b = bufs[h]
        for i, d in enumerate(range(1, NY)):
            arrive(b.brk.at[pl.ds(lax.rem(y + NY - d, NY) * NX, NX)], sems[h].bks, i)

        @pl.loop(0, NX)
        def _(col):
            sums = [jnp.zeros((BLOCK, HD), F32) for _ in range(QB)]
            for r in range(NY):
                term = b.brk[r * NX + col].astype(F32)
                local = jnp.full((BLOCK, HD), tk[r * NX + col], jnp.int32)
                for i in range(QB):
                    sums[i] = sums[i] + jnp.where(local == i, term, 0.0)
            for i in range(QB):
                b.ak[col, i * BLOCK : (i + 1) * BLOCK] = sums[i].astype(BF16)

        for i, d in enumerate(range(1, NX)):
            send(b.ak.at[lax.rem(x + d, NX)], b.rak.at[x], sems[h].axs, i, row_peers[i])
        b.rak[x] = b.ak[x]

    def ring_step(h, s):
        b = bufs[h]
        rows = slice(0, half) if s == 1 else slice(0, TOK)
        arrive(b.ru.at[s - 1, rows], sems[h].bup, s - 1)
        ahead, behind = 6 - s, (6 + s) % NY
        b.su[s, rows] = (b.av[ahead, rows] + b.ru[s - 1, rows].astype(F32)).astype(BF16)
        if s == 1:
            b.su[s, half:TOK] = b.av[ahead, half:TOK].astype(BF16)
        send(b.su.at[s], b.ru.at[s], sems[h].bup, s, up)
        rows = slice(half, TOK) if s == 1 else slice(0, TOK)
        arrive(b.rd.at[s - 1, rows], sems[h].bdown, s - 1)
        b.sd[s, rows] = (b.av[behind, rows] + b.rd[s - 1, rows].astype(F32)).astype(BF16)
        if s == 1:
            b.sd[s, 0:half] = b.av[behind, 0:half].astype(BF16)
        send(b.sd.at[s], b.rd.at[s], sems[h].bdown, s, down)

    def finish(h):
        b = bufs[h]
        cols = slice(h * HD, (h + 1) * HD)
        for i in range(4):
            arrive(b.rim_in.at[i // 2, i % 2], sems[h].rim, i)
        for i, d in enumerate(range(1, NX)):
            arrive(b.rak.at[lax.rem(x + NX - d, NX)], sems[h].axs, i)
        keys = b.wk[BLOCK : BLOCK + TOK]
        for c in range(NX):
            keys = keys + b.rak[c].astype(F32)
        last = slice(TOK - BLOCK, TOK)
        kg_ref[:, cols] = keys.astype(BF16)
        kg_ref[0:BLOCK, cols] = (keys[0:BLOCK] + b.rim_in[0, 0].astype(F32)).astype(BF16)
        kg_ref[last, cols] = (keys[last] + b.rim_in[1, 0].astype(F32)).astype(BF16)
        arrive(b.ru.at[3], sems[h].bup, 3)
        arrive(b.rd.at[3], sems[h].bdown, 3)
        vals = b.wv[BLOCK : BLOCK + TOK] + b.av[2] + b.ru[3].astype(F32) + b.rd[3].astype(F32)
        vg_ref[:, cols] = vals.astype(BF16)
        vg_ref[0:BLOCK, cols] = (vals[0:BLOCK] + b.rim_in[0, 1].astype(F32)).astype(BF16)
        vg_ref[last, cols] = (vals[last] + b.rim_in[1, 1].astype(F32)).astype(BF16)

    for h, b in enumerate(bufs):
        for i, d in enumerate(range(1, NY)):
            arrive(b.rk.at[pl.ds(lax.rem(y + NY - d, NY) * NX, NX)], sems[h].ks, i)
        for i, d in enumerate(range(1, NX)):
            col = lax.rem(x + NX - d, NX) * NY
            arrive(b.rv.at[pl.ds(col, NEAR)], sems[h].vn, i)
            arrive(b.rv.at[pl.ds(col + NEAR, NY - NEAR)], sems[h].vf, i)
        compute(h)
        pack_back(h)
        values_back(h)
        keys_back(h, ROW_ORDER if h == 0 else ROW_ORDER[:2])
    keys_back(1, ROW_ORDER[2:])
    for h in range(KVH):
        rims_back(h)
    reduce_values(0, False)
    reduce_values(1, False)
    reduce_values(0, True)
    ring_step(0, 1)
    ring_step(1, 1)
    reduce_keys(0)
    reduce_values(1, True)
    ring_step(0, 2)
    ring_step(1, 2)
    reduce_keys(1)
    ring_step(0, 3)
    ring_step(1, 3)
    for h in range(KVH):
        finish(h)
    for c in started:
        c.wait_send()


def store(*refs):
    copies = [pltpu.make_async_copy(refs[i], refs[4 + i], refs[8].at[i]) for i in range(4)]
    for c in copies:
        c.start()
    for c in copies:
        c.wait()


def local(queries, keys, values, out_grad, rand_blocks, global_blocks):
    vmem = pl.BlockSpec(memory_space=pltpu.VMEM)
    smem = pl.BlockSpec(memory_space=pltpu.SMEM)
    hbm = pl.BlockSpec(memory_space=pl.ANY)
    sems = []
    for _ in range(KVH):
        for _, n in HEAD_COPIES:
            sems += [pltpu.SemaphoreType.DMA((n,))] * 2
    shapes = [queries.shape, queries.shape, keys.shape, keys.shape]
    held = pl.pallas_call(
        kernel,
        out_shape=tuple(pltpu.VMEM(shape, BF16) for shape in shapes),
        in_specs=[smem, smem, hbm, vmem, vmem, hbm],
        out_specs=(vmem, vmem, vmem, vmem),
        scratch_shapes=[
            pltpu.SMEM((NY * NX,), jnp.int32),
            pltpu.SMEM((NX * NY,), jnp.int32),
            pltpu.SMEM((NY * NX,), jnp.int32),
            pltpu.VMEM((2, 2, BLOCK, KVH * HD), BF16),
            pltpu.VMEM((KEYS, HD), BF16),
            pltpu.VMEM((KEYS, HD), BF16),
            pltpu.VMEM(queries.shape, BF16),
            pltpu.VMEM(queries.shape, BF16),
            pltpu.SemaphoreType.DMA((2,)),
            *[pltpu.VMEM(shape, dtype) for _ in range(KVH) for _, shape, dtype in HEAD_BUFFERS],
            pltpu.SemaphoreType.DMA((4,)),
            pltpu.SemaphoreType.DMA((4,)),
            *sems,
        ],
        compiler_params=pltpu.CompilerParams(collective_id=0, has_side_effects=True),
        name="genome_attention",
    )(rand_blocks.T, global_blocks, queries, keys, values, out_grad)
    return pl.pallas_call(
        store,
        out_shape=tuple(jax.ShapeDtypeStruct(shape, BF16) for shape in shapes),
        in_specs=[vmem] * 4,
        out_specs=(hbm,) * 4,
        scratch_shapes=[pltpu.SemaphoreType.DMA((4,))],
        name="store_outputs",
    )(*[pltpu.with_memory_space_constraint(array, pltpu.VMEM) for array in held])


def solution(mesh):
    tokens, parts = P(("dp", "seq"), None), P("dp", None)
    return jax.shard_map(
        local,
        mesh=mesh,
        in_specs=(tokens, tokens, tokens, tokens, parts, P("dp")),
        out_specs=(tokens, tokens, tokens, tokens),
        check_vma=False,
    )
```

```python
import math

import jax
import jax.numpy as jnp
from jax import lax
from jax.experimental import pallas as pl
from jax.experimental.pallas import tpu as pltpu
from jax.sharding import PartitionSpec as P

KVH = 2
HD = 128
BLOCK = 64
GLOB = 2
RAND = 3
GROUP = 4
QB = 4
NY = 8
NX = 4
NEAR = 5
ROW_ORDER = (4, 3, 5, 2, 6, 1, 7)
FAR = RAND * QB + GLOB
KEYS = (3 + GLOB + RAND) * BLOCK
TOK = QB * BLOCK
SCALE = HD ** (-0.5)
LOG2E = math.log2(math.e)
F32 = jnp.float32
BF16 = jnp.bfloat16


def dot_nt(a, b):
    return lax.dot_general(a, b, (((1,), (1,)), ((), ())), preferred_element_type=F32)


def dot_nn(a, b):
    return lax.dot_general(a, b, (((1,), (0,)), ((), ())), preferred_element_type=F32)


def dot_tn(a, b):
    return lax.dot_general(a, b, (((0,), (0,)), ((), ())), preferred_element_type=F32)


HEAD_BUFFERS = (
    ("xg", (NX * QB, BLOCK, HD), BF16),
    ("yn", (NEAR * QB, BLOCK, HD), BF16),
    ("yf", ((NY - NEAR) * QB, BLOCK, HD), BF16),
    ("sk", (NY * NX, BLOCK, HD), BF16),
    ("rk", (NY * NX, BLOCK, HD), BF16),
    ("sv", (NX * NY, BLOCK, HD), BF16),
    ("rv", (NX * NY, BLOCK, HD), BF16),
    ("fk", (FAR, BLOCK, HD), BF16),
    ("fv", (FAR, BLOCK, HD), BF16),
    ("bsk", (NY * NX, BLOCK, HD), BF16),
    ("brk", (NY * NX, BLOCK, HD), BF16),
    ("bsv", (NX * NY, BLOCK, HD), BF16),
    ("brv", (NX * NY, BLOCK, HD), BF16),
    ("ak", (NX, TOK, HD), BF16),
    ("rak", (NX, TOK, HD), BF16),
    ("av", (NY, TOK, HD), F32),
    ("su", (4, TOK, HD), BF16),
    ("ru", (4, TOK, HD), BF16),
    ("sd", (4, TOK, HD), BF16),
    ("rd", (4, TOK, HD), BF16),
    ("kx", ((QB + 2) * BLOCK, HD), BF16),
    ("vx", ((QB + 2) * BLOCK, HD), BF16),
    ("wk", ((QB + 2) * BLOCK, HD), F32),
    ("wv", ((QB + 2) * BLOCK, HD), F32),
    ("gk", (GLOB * BLOCK, HD), F32),
    ("gv", (GLOB * BLOCK, HD), F32),
    ("rim_out", (2, 2, BLOCK, HD), BF16),
    ("rim_in", (2, 2, BLOCK, HD), BF16),
)
HEAD_COPIES = (
    ("xs", NX - 1), ("up", 4), ("down", 4), ("ks", NY - 1), ("vn", NX - 1), ("vf", NX - 1),
    ("bks", NY - 1), ("bvn", NX - 1), ("bvf", NX - 1), ("axs", NX - 1), ("bup", 4), ("bdown", 4), ("rim", 4),
)


class Named:
    def __init__(self, names, refs):
        for name, ref in zip(names, refs, strict=True):
            setattr(self, name, ref)


def kernel(rb, gb, q_hbm, k_ref, v_ref, g_hbm, out_ref, qg_ref, kg_ref, vg_ref, *scratch):
    scratch = list(scratch)

    def take(n):
        got = scratch[:n]
        del scratch[:n]
        return got

    tk, tv, ent, halo, kc, vc, q_ref, g_ref, load_sems = take(9)
    bufs = [Named([b[0] for b in HEAD_BUFFERS], take(len(HEAD_BUFFERS))) for _ in range(KVH)]
    halo_sems = take(2)
    sems = []
    for _ in range(KVH):
        refs = take(2 * len(HEAD_COPIES))
        sems.append(Named([c[0] for c in HEAD_COPIES], [(refs[2 * i], refs[2 * i + 1]) for i in range(len(HEAD_COPIES))]))

    me = lax.axis_index("seq")
    y, x = lax.div(me, NX), lax.rem(me, NX)

    def at(row, col):
        return lax.rem(row, NY) * NX + lax.rem(col, NX)

    col_peers = [at(y + d, x) for d in range(1, NY)]
    row_peers = [at(y, x + d) for d in range(1, NX)]
    up, down = at(y + 1, x), at(y + NY - 1, x)
    after = lax.rem(me + 1, NY * NX)
    before = lax.rem(me + NY * NX - 1, NY * NX)
    barrier = pltpu.get_barrier_semaphore()
    peers = col_peers + row_peers + [after, before]
    for peer in peers:
        pl.semaphore_signal(barrier, inc=1, device_id={"seq": peer}, device_id_type=pl.DeviceIdType.MESH)

    loads = [pltpu.make_async_copy(q_hbm, q_ref, load_sems.at[0]), pltpu.make_async_copy(g_hbm, g_ref, load_sems.at[1])]
    for c in loads:
        c.start()
    started = []

    def copy(src, dst, pair, i, peer):
        return pltpu.make_async_remote_copy(
            src_ref=src, dst_ref=dst, send_sem=pair[0].at[i], recv_sem=pair[1].at[i],
            device_id={"seq": peer}, device_id_type=pl.DeviceIdType.MESH,
        )

    def send(src, dst, pair, i, peer):
        c = copy(src, dst, pair, i, peer)
        c.start()
        started.append(c)

    def arrive(dst, pair, i):
        copy(dst, dst, pair, i, after).wait_recv()

    for h, b in enumerate(bufs):
        cols = slice(h * HD, (h + 1) * HD)
        b.xg[pl.ds(x * QB, QB)] = k_ref[:, cols].reshape(QB, BLOCK, HD)
        b.yn[2 * QB : 3 * QB] = v_ref[:, cols].reshape(QB, BLOCK, HD)
        b.kx[BLOCK : BLOCK + TOK] = k_ref[:, cols]
        b.vx[BLOCK : BLOCK + TOK] = v_ref[:, cols]

    pl.semaphore_wait(barrier, len(peers))

    def held(b, i, first=0, n=QB):
        ref, i = (b.yn, i) if i < NEAR else (b.yf, i - NEAR)
        return ref.at[i * QB + first : i * QB + first + n]

    def ring_out(h, s):
        b = bufs[h]
        n = QB if s < 3 else QB // 2
        send(held(b, (2 - s) % NY, 0, n), held(b, (1 - s) % NY, 0, n), sems[h].up, s, up)
        send(held(b, 2 + s, QB - n, n), held(b, 3 + s, QB - n, n), sems[h].down, s, down)

    def ring_in(h, s):
        b = bufs[h]
        n = QB if s < 3 else QB // 2
        arrive(held(b, (1 - s) % NY, 0, n), sems[h].up, s)
        arrive(held(b, 3 + s, QB - n, n), sems[h].down, s)

    send(k_ref.at[TOK - BLOCK : TOK], halo.at[0, 0], halo_sems, 0, after)
    send(v_ref.at[TOK - BLOCK : TOK], halo.at[0, 1], halo_sems, 1, after)
    send(k_ref.at[0:BLOCK], halo.at[1, 0], halo_sems, 2, before)
    send(v_ref.at[0:BLOCK], halo.at[1, 1], halo_sems, 3, before)
    for h in range(KVH):
        ring_out(h, 0)
    for h, b in enumerate(bufs):
        own = b.xg.at[pl.ds(x * QB, QB)]
        for i, peer in enumerate(row_peers):
            send(own, own, sems[h].xs, i, peer)

    def listed(device):
        ids = [rb[e % RAND, device * QB + e // RAND] for e in range(RAND * QB)]
        return ids + [gb[e] for e in range(GLOB)]

    def named(ids, owner, pick):
        found = jnp.int32(-1)
        for e, block in enumerate(ids):
            found = jnp.where((block >> 2) == owner, pick(e, block), found)
        return found

    @pl.loop(0, NY)
    def _(row):
        ids = listed(row * NX + x)
        for c in range(NX):
            tk[row * NX + c] = named(ids, y * NX + c, lambda e, block: block & 3)

    @pl.loop(0, NX)
    def _(col):
        ids = listed(y * NX + col)
        for i in range(NY):
            owner = lax.rem(y + i + NY - 2, NY) * NX + x
            tv[col * NY + i] = named(ids, owner, lambda e, block: block & 3)

    mine = listed(me)

    @pl.loop(0, NY * NX)
    def _(owner):
        ent[owner] = jnp.maximum(named(mine, owner, lambda e, block: jnp.int32(e)), 0)

    half = TOK // 2

    def send_keys(h):
        b = bufs[h]
        for i, d in enumerate(range(1, NX)):
            arrive(b.xg.at[pl.ds(lax.rem(x + NX - d, NX) * QB, QB)], sems[h].xs, i)

        @pl.loop(0, NY)
        def _(row):
            for c in range(NX):
                b.sk[row * NX + c] = b.xg[c * QB + jnp.maximum(tk[row * NX + c], 0)]

        for d in ROW_ORDER:
            row = lax.rem(y + d, NY)
            send(b.sk.at[pl.ds(row * NX, NX)], b.rk.at[pl.ds(y * NX, NX)], sems[h].ks, d - 1, col_peers[d - 1])
        b.rk[pl.ds(y * NX, NX)] = b.sk[pl.ds(y * NX, NX)]

    def send_values(h, near):
        b = bufs[h]
        first, n = (0, NEAR) if near else (NEAR, NY - NEAR)
        ref = b.yn if near else b.yf

        @pl.loop(0, NX)
        def _(col):
            for i in range(n):
                b.sv[col * NY + first + i] = ref[i * QB + jnp.maximum(tv[col * NY + first + i], 0)]

        for i, d in enumerate(range(1, NX)):
            col = lax.rem(x + d, NX)
            send(
                b.sv.at[pl.ds(col * NY + first, n)], b.rv.at[pl.ds(x * NY + first, n)],
                sems[h].vn if near else sems[h].vf, i, row_peers[i],
            )
        b.rv[pl.ds(x * NY + first, n)] = b.sv[pl.ds(x * NY + first, n)]

    for s in range(2):
        for h in range(KVH):
            ring_in(h, s)
            ring_out(h, s + 1)
    send_values(0, True)
    for h in range(KVH):
        ring_in(h, 2)
        ring_out(h, 3)
    send_keys(0)
    ring_in(0, 3)
    send_values(0, False)
    send_values(1, True)
    ring_in(1, 3)
    send_values(1, False)
    send_keys(1)

    for i in range(4):
        arrive(halo.at[i // 2, i % 2], halo_sems, i)
    for h, b in enumerate(bufs):
        cols = slice(h * HD, (h + 1) * HD)
        b.kx[0:BLOCK] = halo[0, 0, :, cols]
        b.vx[0:BLOCK] = halo[0, 1, :, cols]
        b.kx[BLOCK + TOK :] = halo[1, 0, :, cols]
        b.vx[BLOCK + TOK :] = halo[1, 1, :, cols]

    for c in loads:
        c.wait()

    def compute(h):
        b = bufs[h]
        for ref in (b.wk, b.wv, b.gk, b.gv):
            ref[...] = jnp.zeros_like(ref)
        window, globe = 3 * BLOCK, GLOB * BLOCK
        for i in range(GLOB):
            owner = gb[i] >> 2
            kc[window + i * BLOCK : window + (i + 1) * BLOCK] = b.rk[owner]
            vc[window + i * BLOCK : window + (i + 1) * BLOCK] = b.rv[(owner & 3) * NY + (((owner >> 2) + NY + 2 - y) & 7)]

        @pl.loop(0, QB)
        def _(j):
            rows = pl.ds(pl.multiple_of(j * BLOCK, BLOCK), BLOCK)
            span = pl.ds(pl.multiple_of(j * BLOCK, BLOCK), window)
            kc[0:window] = b.kx[span]
            vc[0:window] = b.vx[span]
            for i in range(RAND):
                owner = rb[i, me * QB + j] >> 2
                to = slice(window + globe + i * BLOCK, window + globe + (i + 1) * BLOCK)
                kc[to] = b.rk[owner]
                vc[to] = b.rv[(owner & 3) * NY + (((owner >> 2) + NY + 2 - y) & 7)]
            base = h * GROUP * HD
            q = jnp.concatenate([q_ref[rows, base + i * HD : base + (i + 1) * HD] for i in range(GROUP)], axis=0)
            g = jnp.concatenate([g_ref[rows, base + i * HD : base + (i + 1) * HD] for i in range(GROUP)], axis=0)
            k, v = kc[...], vc[...]
            scores = dot_nt(q, k)
            peak = jnp.max(scores, axis=1, keepdims=True)
            expos = jnp.exp2((scores - peak) * (SCALE * LOG2E))
            probs = expos * (1.0 / jnp.sum(expos, axis=1, keepdims=True))
            probs_b = probs.astype(BF16)
            attended = dot_nn(probs_b, v)
            delta = jnp.sum(g.astype(F32) * attended, axis=1, keepdims=True)
            dprobs = dot_nt(g, v)
            dscores = (probs * (dprobs - delta)).astype(BF16)
            qgrad = dot_nn(dscores, k) * SCALE
            for i in range(GROUP):
                part = slice(i * BLOCK, (i + 1) * BLOCK)
                out_ref[rows, base + i * HD : base + (i + 1) * HD] = attended[part].astype(BF16)
                qg_ref[rows, base + i * HD : base + (i + 1) * HD] = qgrad[part].astype(BF16)
            key_part = dot_tn(dscores, q) * SCALE
            b.wk[span] += key_part[:window]
            b.gk[...] += key_part[window : window + globe]
            b.fk[pl.ds(j * RAND, RAND)] = key_part[window + globe :].astype(BF16).reshape(RAND, BLOCK, HD)
            value_part = dot_tn(probs_b, g)
            b.wv[span] += value_part[:window]
            b.gv[...] += value_part[window : window + globe]
            b.fv[pl.ds(j * RAND, RAND)] = value_part[window + globe :].astype(BF16).reshape(RAND, BLOCK, HD)

        b.fk[RAND * QB :] = b.gk[...].astype(BF16).reshape(GLOB, BLOCK, HD)
        b.fv[RAND * QB :] = b.gv[...].astype(BF16).reshape(GLOB, BLOCK, HD)

    def pack_values_back(h):
        b = bufs[h]

        @pl.loop(0, NX)
        def _(col):
            for i in range(NY):
                b.bsv[col * NY + i] = b.fv[ent[lax.rem(y + i + NY - 2, NY) * NX + col]]

    def pack_keys_back(h):
        b = bufs[h]

        @pl.loop(0, NY)
        def _(row):
            for c in range(NX):
                b.bsk[row * NX + c] = b.fk[ent[row * NX + c]]

    def values_back(h):
        b = bufs[h]
        for near in (False, True):
            first, n = (0, NEAR) if near else (NEAR, NY - NEAR)
            for i, d in enumerate(range(1, NX)):
                col = lax.rem(x + d, NX)
                send(
                    b.bsv.at[pl.ds(col * NY + first, n)], b.brv.at[pl.ds(x * NY + first, n)],
                    sems[h].bvn if near else sems[h].bvf, i, row_peers[i],
                )
        b.brv[pl.ds(x * NY, NY)] = b.bsv[pl.ds(x * NY, NY)]

    def keys_back(h, distances):
        b = bufs[h]
        for d in distances:
            row = lax.rem(y + d, NY)
            send(b.bsk.at[pl.ds(row * NX, NX)], b.brk.at[pl.ds(y * NX, NX)], sems[h].bks, d - 1, col_peers[d - 1])
        if distances[-1] == ROW_ORDER[-1]:
            b.brk[pl.ds(y * NX, NX)] = b.bsk[pl.ds(y * NX, NX)]

    def rims_back(h):
        b = bufs[h]
        b.rim_out[0, 0] = b.wk[(QB + 1) * BLOCK :].astype(BF16)
        b.rim_out[0, 1] = b.wv[(QB + 1) * BLOCK :].astype(BF16)
        b.rim_out[1, 0] = b.wk[0:BLOCK].astype(BF16)
        b.rim_out[1, 1] = b.wv[0:BLOCK].astype(BF16)
        for i in range(4):
            send(b.rim_out.at[i // 2, i % 2], b.rim_in.at[i // 2, i % 2], sems[h].rim, i, after if i < 2 else before)

    def reduce_values(h, near):
        b = bufs[h]
        first, n = (0, NEAR) if near else (NEAR, NY - NEAR)
        for i, d in enumerate(range(1, NX)):
            arrive(
                b.brv.at[pl.ds(lax.rem(x + NX - d, NX) * NY + first, n)],
                sems[h].bvn if near else sems[h].bvf, i,
            )

        @pl.loop(first, first + n)
        def _(row):
            sums = [jnp.zeros((BLOCK, HD), F32) for _ in range(QB)]
            for c in range(NX):
                term = b.brv[c * NY + row].astype(F32)
                local = jnp.full((BLOCK, HD), tv[c * NY + row], jnp.int32)
                for i in range(QB):
                    sums[i] = sums[i] + jnp.where(local == i, term, 0.0)
            for i in range(QB):
                b.av[row, i * BLOCK : (i + 1) * BLOCK] = sums[i]

        if not near:
            b.su[0, 0:half] = b.av[6, 0:half].astype(BF16)
            b.sd[0, half:TOK] = b.av[6, half:TOK].astype(BF16)
            send(b.su.at[0, 0:half], b.ru.at[0, 0:half], sems[h].bup, 0, up)
            send(b.sd.at[0, half:TOK], b.rd.at[0, half:TOK], sems[h].bdown, 0, down)

    def reduce_keys(h):
        b = bufs[h]
        for i, d in enumerate(range(1, NY)):
            arrive(b.brk.at[pl.ds(lax.rem(y + NY - d, NY) * NX, NX)], sems[h].bks, i)

        @pl.loop(0, NX)
        def _(col):
            sums = [jnp.zeros((BLOCK, HD), F32) for _ in range(QB)]
            for r in range(NY):
                term = b.brk[r * NX + col].astype(F32)
                local = jnp.full((BLOCK, HD), tk[r * NX + col], jnp.int32)
                for i in range(QB):
                    sums[i] = sums[i] + jnp.where(local == i, term, 0.0)
            for i in range(QB):
                b.ak[col, i * BLOCK : (i + 1) * BLOCK] = sums[i].astype(BF16)

        for i, d in enumerate(range(1, NX)):
            send(b.ak.at[lax.rem(x + d, NX)], b.rak.at[x], sems[h].axs, i, row_peers[i])
        b.rak[x] = b.ak[x]

    def ring_step(h, s):
        b = bufs[h]
        rows = slice(0, half) if s == 1 else slice(0, TOK)
        arrive(b.ru.at[s - 1, rows], sems[h].bup, s - 1)
        ahead, behind = 6 - s, (6 + s) % NY
        b.su[s, rows] = (b.av[ahead, rows] + b.ru[s - 1, rows].astype(F32)).astype(BF16)
        if s == 1:
            b.su[s, half:TOK] = b.av[ahead, half:TOK].astype(BF16)
        send(b.su.at[s], b.ru.at[s], sems[h].bup, s, up)
        rows = slice(half, TOK) if s == 1 else slice(0, TOK)
        arrive(b.rd.at[s - 1, rows], sems[h].bdown, s - 1)
        b.sd[s, rows] = (b.av[behind, rows] + b.rd[s - 1, rows].astype(F32)).astype(BF16)
        if s == 1:
            b.sd[s, 0:half] = b.av[behind, 0:half].astype(BF16)
        send(b.sd.at[s], b.rd.at[s], sems[h].bdown, s, down)

    def finish(h):
        b = bufs[h]
        cols = slice(h * HD, (h + 1) * HD)
        for i in range(4):
            arrive(b.rim_in.at[i // 2, i % 2], sems[h].rim, i)
        for i, d in enumerate(range(1, NX)):
            arrive(b.rak.at[lax.rem(x + NX - d, NX)], sems[h].axs, i)
        keys = b.wk[BLOCK : BLOCK + TOK]
        for c in range(NX):
            keys = keys + b.rak[c].astype(F32)
        last = slice(TOK - BLOCK, TOK)
        kg_ref[:, cols] = keys.astype(BF16)
        kg_ref[0:BLOCK, cols] = (keys[0:BLOCK] + b.rim_in[0, 0].astype(F32)).astype(BF16)
        kg_ref[last, cols] = (keys[last] + b.rim_in[1, 0].astype(F32)).astype(BF16)
        arrive(b.ru.at[3], sems[h].bup, 3)
        arrive(b.rd.at[3], sems[h].bdown, 3)
        vals = b.wv[BLOCK : BLOCK + TOK] + b.av[2] + b.ru[3].astype(F32) + b.rd[3].astype(F32)
        vg_ref[:, cols] = vals.astype(BF16)
        vg_ref[0:BLOCK, cols] = (vals[0:BLOCK] + b.rim_in[0, 1].astype(F32)).astype(BF16)
        vg_ref[last, cols] = (vals[last] + b.rim_in[1, 1].astype(F32)).astype(BF16)

    for h, b in enumerate(bufs):
        for i, d in enumerate(range(1, NY)):
            arrive(b.rk.at[pl.ds(lax.rem(y + NY - d, NY) * NX, NX)], sems[h].ks, i)
        for i, d in enumerate(range(1, NX)):
            col = lax.rem(x + NX - d, NX) * NY
            arrive(b.rv.at[pl.ds(col, NEAR)], sems[h].vn, i)
            arrive(b.rv.at[pl.ds(col + NEAR, NY - NEAR)], sems[h].vf, i)
        compute(h)
        pack_values_back(h)
        values_back(h)
        pack_keys_back(h)
        keys_back(h, ROW_ORDER if h == 0 else ROW_ORDER[:2])
    keys_back(1, ROW_ORDER[2:])
    for h in range(KVH):
        rims_back(h)
    reduce_values(0, False)
    reduce_values(1, False)
    reduce_values(0, True)
    ring_step(0, 1)
    ring_step(1, 1)
    reduce_keys(0)
    reduce_values(1, True)
    ring_step(0, 2)
    ring_step(1, 2)
    reduce_keys(1)
    ring_step(0, 3)
    ring_step(1, 3)
    for h in range(KVH):
        finish(h)
    for c in started:
        c.wait_send()


def store(*refs):
    copies = [pltpu.make_async_copy(refs[i], refs[4 + i], refs[8].at[i]) for i in range(4)]
    for c in copies:
        c.start()
    for c in copies:
        c.wait()


def local(queries, keys, values, out_grad, rand_blocks, global_blocks):
    vmem = pl.BlockSpec(memory_space=pltpu.VMEM)
    smem = pl.BlockSpec(memory_space=pltpu.SMEM)
    hbm = pl.BlockSpec(memory_space=pl.ANY)
    sems = []
    for _ in range(KVH):
        for _, n in HEAD_COPIES:
            sems += [pltpu.SemaphoreType.DMA((n,))] * 2
    shapes = [queries.shape, queries.shape, keys.shape, keys.shape]
    held = pl.pallas_call(
        kernel,
        out_shape=tuple(pltpu.VMEM(shape, BF16) for shape in shapes),
        in_specs=[smem, smem, hbm, vmem, vmem, hbm],
        out_specs=(vmem, vmem, vmem, vmem),
        scratch_shapes=[
            pltpu.SMEM((NY * NX,), jnp.int32),
            pltpu.SMEM((NX * NY,), jnp.int32),
            pltpu.SMEM((NY * NX,), jnp.int32),
            pltpu.VMEM((2, 2, BLOCK, KVH * HD), BF16),
            pltpu.VMEM((KEYS, HD), BF16),
            pltpu.VMEM((KEYS, HD), BF16),
            pltpu.VMEM(queries.shape, BF16),
            pltpu.VMEM(queries.shape, BF16),
            pltpu.SemaphoreType.DMA((2,)),
            *[pltpu.VMEM(shape, dtype) for _ in range(KVH) for _, shape, dtype in HEAD_BUFFERS],
            pltpu.SemaphoreType.DMA((4,)),
            pltpu.SemaphoreType.DMA((4,)),
            *sems,
        ],
        compiler_params=pltpu.CompilerParams(collective_id=0, has_side_effects=True),
        name="genome_attention",
    )(rand_blocks.T, global_blocks, queries, keys, values, out_grad)
    return pl.pallas_call(
        store,
        out_shape=tuple(jax.ShapeDtypeStruct(shape, BF16) for shape in shapes),
        in_specs=[vmem] * 4,
        out_specs=(hbm,) * 4,
        scratch_shapes=[pltpu.SemaphoreType.DMA((4,))],
        name="store_outputs",
    )(*[pltpu.with_memory_space_constraint(array, pltpu.VMEM) for array in held])


def solution(mesh):
    tokens, parts = P(("dp", "seq"), None), P("dp", None)
    return jax.shard_map(
        local,
        mesh=mesh,
        in_specs=(tokens, tokens, tokens, tokens, parts, P("dp")),
        out_specs=(tokens, tokens, tokens, tokens),
        check_vma=False,
    )
```
